256 devices in a mesh: seq: 32 (over z, x), head: 8 (over y, core).
Axes of the slice: x: 4, y: 4, z: 8, core: 2. Of those that a mesh axis runs over, the one named last changes fastest.
Arguments:
- queries: bfloat16 [32768, 4096], P('seq', 'head'), may hold values from -6 to 6
- key_rows: bfloat16 [32768, 4096], P('seq', 'head'), may hold values from -6 to 6
- value_rows: bfloat16 [32768, 4096], P('seq', 'head'), may hold values from -6 to 6
- out_grad: bfloat16 [32768, 4096], P('seq', 'head'), may hold values from -6 to 6
- cache_states: bfloat16 [32, 32, 128, 128], P('seq', 'head'), may hold values from -96 to 96
- session_start: int32 [32], P('seq'), may hold values from 0 to 1024, as said below
- cache_owner: int32 [32], replicated, may hold values from 0 to 31, as said below
- probe_gate: float32 [32768], P('seq'), may hold values from 0.1 to 4.5
- steer_vector: bfloat16 [32, 128], P('head'), may hold values from -0.09375 to 0.09375
Outputs:
- grad_queries: bfloat16 [32768, 4096], P('seq', 'head')
- grad_keys: bfloat16 [32768, 4096], P('seq', 'head')
- grad_values: bfloat16 [32768, 4096], P('seq', 'head')
- grad_cache: bfloat16 [32, 32, 128, 128], P('seq', 'head')
- grad_steer: float32 [32, 128], P('head')
- grad_gate: float32 [32768], P('seq')
The draws below stay inside these ranges and needn't reach their ends.
Inputs may be any that keep to these rules, and one draw needn't show every extreme that they name: session_start[b] is the position of the session beginning in block b, or 1024 where none does; it is 512 for every b with b % 4 == 3, so no session reaches across more than 5 blocks. `cache_owner`: a permutation of the slots.
All inputs are finite; a program needn't handle non-finite values.
Results may differ from the reference program's by a relative error of at most 0.007.
Values may be sent and summed in bfloat16 or wider, within the bound.
No kernel may reach another device: no remote copies, remote signals or barrier semaphores. Data moves between devices by JAX's collectives and lax.ppermute only.
A program may use at most 128 MiB of HBM per device.

```python
import math
import jax
import jax.numpy as jnp
from jax import lax

HEADS = 32
DK = 128
DV = 128
SPAN = 4
TOK_DEV = 1024
BLOCKS = 32
TOKENS = 32768


def draw_session_start(key, part):
    subkeys = jax.random.split(jax.random.fold_in(key, 101), 3)
    blocks = jnp.arange(BLOCKS)
    chosen = jax.random.randint(subkeys[0], (BLOCKS,), 0, 2) == 1
    places = jax.random.randint(subkeys[1], (BLOCKS,), 1, TOK_DEV)
    vacant_count = jax.random.randint(subkeys[2], (), 1, SPAN)
    middle = BLOCKS // 2
    vacant = (blocks > middle) & (blocks <= middle + vacant_count)
    aligned = blocks % SPAN == SPAN - 1
    result = jnp.where(aligned, TOK_DEV // 2, jnp.where(chosen & jnp.logical_not(vacant), places, TOK_DEV))
    return result.astype(jnp.int32)


def force_slot(order, block_pos, wanted):
    slots = jnp.arange(BLOCKS, dtype=jnp.int32)
    holder = jnp.argmax(order == wanted).astype(jnp.int32)
    current = order[block_pos]
    order = jnp.where(slots == holder, current, order)
    order = jnp.where(slots == block_pos, wanted, order)
    return order.astype(jnp.int32)


def draw_cache_owner(key, part):
    subkeys = jax.random.split(jax.random.fold_in(key, 202), 2)
    order = jax.random.permutation(subkeys[0], BLOCKS).astype(jnp.int32)
    first_block = (jax.random.randint(subkeys[1], (), 0, BLOCKS // SPAN) * SPAN + SPAN - 1).astype(jnp.int32)
    second_block = ((first_block + SPAN) % BLOCKS).astype(jnp.int32)
    first_wanted = ((first_block + BLOCKS // 2) % BLOCKS).astype(jnp.int32)
    second_wanted = ((second_block + BLOCKS - 1) % BLOCKS).astype(jnp.int32)
    order = force_slot(order, first_block, first_wanted)
    order = force_slot(order, second_block, second_wanted)
    return order.astype(jnp.int32)


def draw_probe_gate(key, part):
    subkey = jax.random.fold_in(key, 303)
    position_ramp = 1.0 + 2.0 * jnp.arange(TOKENS, dtype=jnp.float32) / (TOKENS - 1)
    factor = jax.random.uniform(subkey, (TOKENS,), jnp.float32, 0.5, 1.5)
    return (factor * position_ramp).astype(jnp.float32)


def steps_of(stream_key, shape, pieces, smallest, largest):
    def one(position, parts):
        heights = jax.random.uniform(jax.random.fold_in(jax.random.fold_in(stream_key, 6), position), (parts,), jnp.float32, smallest / len(pieces), largest / len(pieces))
        return jnp.repeat(jnp.exp(heights), shape[position] // parts).reshape((-1,) + (1,) * (len(shape) - position - 1))

    factor_of = one(*pieces[0])
    for cut in pieces[1:]:
        factor_of = factor_of * one(*cut)
    return factor_of


def centred(own_key, dims, spread, limit, cuts=(), held_as=jnp.bfloat16):
    values = jax.random.normal(own_key, dims, jnp.float32) * spread
    if len(cuts) > 0:
        values = steps_of(own_key, dims, cuts, -0.22, 0.18) * values
    return jnp.clip(values, min=-limit, max=limit).astype(held_as)


def setup_inputs(seed: int = 0) -> dict:
    arg_keys = jax.random.split(jax.random.key(seed), 10)
    queries = centred(arg_keys[0], (TOKENS, HEADS * DK), 1.0, 6.0, ((0, 32), (1, 8)))
    key_rows = centred(arg_keys[1], (TOKENS, HEADS * DK), 1.0, 6.0, ((0, 32), (1, 8)))
    value_rows = centred(arg_keys[2], (TOKENS, HEADS * DV), 1.0, 6.0, ((0, 32), (1, 8)))
    out_grad = centred(arg_keys[3], (TOKENS, HEADS * DV), 1.0, 6.0, ((0, 32), (1, 8)))
    cache_states = centred(arg_keys[4], (BLOCKS, HEADS, DK, DV), 16.0, 96.0, ((0, 32), (1, 8)))
    session_start = draw_session_start(jax.random.fold_in(arg_keys[9], 71), 0)
    cache_owner = draw_cache_owner(jax.random.fold_in(arg_keys[9], 71), 0)
    probe_gate = draw_probe_gate(jax.random.fold_in(arg_keys[9], 71), 0)
    steer_vector = centred(arg_keys[8], (HEADS, DV), (HEADS * DV) ** -0.5, 0.09375, ((0, 8),))
    return dict(queries=queries, key_rows=key_rows, value_rows=value_rows, out_grad=out_grad, cache_states=cache_states, session_start=session_start, cache_owner=cache_owner, probe_gate=probe_gate, steer_vector=steer_vector)


def rounded(values):
    return lax.optimization_barrier(values.astype(jnp.bfloat16)).astype(jnp.float32)

def block_masks(start_pos):
    positions = jnp.arange(TOK_DEV)
    before_start = positions < start_pos
    after_start = positions >= start_pos
    final_part = after_start | (start_pos >= TOK_DEV)
    causal = (positions[None, :] <= positions[:, None]) & (after_start[:, None] == after_start[None, :])
    return (before_start, after_start, final_part, causal)

def reference(queries, key_rows, value_rows, out_grad, cache_states, session_start, cache_owner, probe_gate, steer_vector):
    scaling = 1.0 / DK
    query_blocks = queries.reshape(BLOCKS, TOK_DEV, HEADS, DK)
    key_blocks = key_rows.reshape(BLOCKS, TOK_DEV, HEADS, DK)
    value_blocks = value_rows.reshape(BLOCKS, TOK_DEV, HEADS, DV)
    grad_blocks = out_grad.reshape(BLOCKS, TOK_DEV, HEADS, DV)
    has_start = session_start < TOK_DEV
    owned_states = cache_states[cache_owner]

    def summarize(block_items):
        query_part, key_part, value_part, grad_part, start_pos = block_items
        query_part = query_part.astype(jnp.float32)
        key_part = key_part.astype(jnp.float32)
        value_part = value_part.astype(jnp.float32)
        grad_part = grad_part.astype(jnp.float32)
        before_start, after_start, final_part, causal = block_masks(start_pos)
        kv_final = jnp.einsum('thd,the->hde', key_part * final_part[:, None, None], value_part)
        head_sum = scaling * jnp.einsum('thd,the->hde', query_part * before_start[:, None, None], grad_part)
        start_sum = scaling * jnp.einsum('thd,the->hde', query_part * after_start[:, None, None], grad_part)
        return (kv_final, head_sum, start_sum)
    kv_finals, head_sums, start_sums = lax.map(summarize, (query_blocks, key_blocks, value_blocks, grad_blocks, session_start))
    start_flags = has_start[:, None, None, None]
    tail_states = jnp.where(start_flags, owned_states.astype(jnp.float32) + kv_finals, kv_finals)

    def advance(running, block_items):
        tail_state, flag_value = block_items
        return (jnp.where(flag_value, tail_state, running + tail_state), running)
    zero_state = jnp.zeros((HEADS, DK, DV), jnp.float32)
    _, entering = lax.scan(advance, zero_state, (tail_states, has_start))
    _, leaving = lax.scan(advance, zero_state, (head_sums, has_start), reverse=True)
    start_grads = jnp.where(start_flags, start_sums + leaving, 0.0).astype(jnp.bfloat16)
    grad_cache = jnp.zeros((BLOCKS, HEADS, DK, DV), jnp.bfloat16).at[cache_owner].set(start_grads)

    def gradients(block_items):
        query_part, key_part, value_part, grad_part, start_pos, enter_state, leave_state, owned_state = block_items
        query_part = query_part.astype(jnp.float32)
        key_part = key_part.astype(jnp.float32)
        value_part = value_part.astype(jnp.float32)
        grad_part = grad_part.astype(jnp.float32)
        before_start, after_start, final_part, causal = block_masks(start_pos)
        grad_scores = rounded(jnp.where(causal[None], scaling * jnp.einsum('she,the->hst', grad_part, value_part), 0.0))
        key_scores = rounded(jnp.where(causal[None], scaling * jnp.einsum('shd,thd->hst', query_part, key_part), 0.0))
        enter_low = rounded(enter_state)
        leave_low = rounded(leave_state)
        owned_wide = owned_state.astype(jnp.float32)
        inter_query = jnp.einsum('she,hde->shd', grad_part * before_start[:, None, None], enter_low)
        inter_query = inter_query + jnp.einsum('she,hde->shd', grad_part * after_start[:, None, None], owned_wide)
        grad_query = jnp.einsum('hst,thd->shd', grad_scores, key_part) + scaling * inter_query
        grad_key = jnp.einsum('hst,shd->thd', grad_scores, query_part)
        grad_key = grad_key + jnp.einsum('the,hde->thd', value_part * final_part[:, None, None], leave_low)
        grad_value = jnp.einsum('hst,she->the', key_scores, grad_part)
        grad_value = grad_value + jnp.einsum('thd,hde->the', key_part * final_part[:, None, None], leave_low)
        return (grad_query.reshape(TOK_DEV, HEADS * DK).astype(jnp.bfloat16), grad_key.reshape(TOK_DEV, HEADS * DK).astype(jnp.bfloat16), grad_value.reshape(TOK_DEV, HEADS * DV).astype(jnp.bfloat16))
    grad_queries, grad_keys, grad_values = lax.map(gradients, (query_blocks, key_blocks, value_blocks, grad_blocks, session_start, entering, leaving, owned_states))
    grad_wide = out_grad.astype(jnp.float32).reshape(TOKENS, HEADS, DV)
    grad_steer = jnp.einsum('t,the->he', probe_gate.astype(jnp.float32), grad_wide) / math.sqrt(TOKENS)
    grad_gate = jnp.einsum('the,he->t', grad_wide, steer_vector.astype(jnp.float32))
    return (grad_queries.reshape(TOKENS, HEADS * DK), grad_keys.reshape(TOKENS, HEADS * DK), grad_values.reshape(TOKENS, HEADS * DV), grad_cache, grad_steer, grad_gate)
```

```python
import functools
import math

import jax
import jax.numpy as jnp
from jax import lax
from jax.experimental import pallas as pl
from jax.experimental.pallas import tpu as pltpu
from jax.sharding import PartitionSpec as P

D = 128
PIECE = 16
STRIP = 256
F32 = jnp.float32
BF16 = jnp.bfloat16


def nt(a, b):
    return lax.dot_general(a, b, (((1,), (1,)), ((), ())), preferred_element_type=F32)


def nn(a, b):
    return lax.dot_general(a, b, (((1,), (0,)), ((), ())), preferred_element_type=F32)


def tn(a, b):
    return lax.dot_general(a, b, (((0,), (0,)), ((), ())), preferred_element_type=F32)


def row_masks(start, length):
    rows = lax.broadcasted_iota(jnp.int32, (length, D), 0)
    after = (rows >= start).astype(F32)
    before = 1.0 - after
    whole = jnp.where(start >= length, 1.0, 0.0).astype(F32)
    final = jnp.maximum(after, whole)
    return before.astype(BF16), after.astype(BF16), final.astype(BF16)


def sums_kernel(start_ref, q_ref, k_ref, v_ref, g_ref, c_ref, probe_ref, steer_ref, u_ref, gate_ref, acc_ref):
    head = pl.program_id(0)
    length = q_ref.shape[0]
    start = start_ref[0]
    before, after, final = row_masks(start, length)
    g = g_ref[...]
    kv = tn(k_ref[...], v_ref[...] * final)
    both = tn(q_ref[...], jnp.concatenate([g * before, g * after], axis=1))
    pieces = D // PIECE
    here = pl.ds(head * pieces, pieces)
    u_ref[here, 0:16, :] = kv.astype(BF16).reshape(pieces, PIECE, D)
    u_ref[here, 16:32, :] = both[:, :D].astype(BF16).reshape(pieces, PIECE, D)
    u_ref[here, 32:48, :] = both[:, D:].astype(BF16).reshape(pieces, PIECE, D)
    u_ref[here, 48:64, :] = c_ref[0, 0].reshape(pieces, PIECE, D)

    probe = probe_ref[...]
    high = probe.astype(BF16)
    low = (probe - high.astype(F32)).astype(BF16)
    steer_sum = nn(high, g) + nn(low, g)
    which = lax.broadcasted_iota(jnp.int32, (8, D), 0) == head
    steer_rows = jnp.where(which, jnp.broadcast_to(steer_sum, (8, D)), 0.0)
    vector = jnp.where(which, steer_ref[...], 0.0).astype(BF16)
    gate_rows = nt(vector, g)
    gate_sum = jnp.sum(gate_rows, axis=0, keepdims=True)

    @pl.when(head == 0)
    def _():
        acc_ref[...] = steer_rows
        gate_ref[...] = gate_sum

    @pl.when(head > 0)
    def _():
        acc_ref[...] += steer_rows
        gate_ref[...] += gate_sum

    @pl.when(head == pl.num_programs(0) - 1)
    def _():
        total = acc_ref[...]
        total_high = total.astype(BF16).astype(F32)
        total_low = total - total_high
        rows = lax.broadcasted_iota(jnp.int32, (8, D), 0)
        spread = jnp.where(rows < 4, total_high, pltpu.roll(total_low, 4, 0))
        flag = jnp.where(start < length, 1.0, 0.0).astype(F32)
        tile = jnp.concatenate([spread, jnp.full((8, D), flag)], axis=0).astype(BF16)
        u_ref[:, 64:80, :] = jnp.broadcast_to(tile[None], (u_ref.shape[0], PIECE, D))


def block_sums(queries, key_rows, value_rows, out_grad, cache_states, session_start, probe_gate, steer_vector):
    length, width = queries.shape
    heads = width // D
    total = heads * D // PIECE
    steer_rows = jnp.zeros((8, D), F32).at[:heads].set(steer_vector.astype(F32))
    column = pl.BlockSpec((length, D), lambda h: (0, h))
    return pl.pallas_call(
        sums_kernel,
        grid=(heads,),
        in_specs=[
            pl.BlockSpec(memory_space=pltpu.SMEM),
            column,
            column,
            column,
            column,
            pl.BlockSpec((1, 1, D, D), lambda h: (0, h, 0, 0)),
            pl.BlockSpec((1, length), lambda h: (0, 0)),
            pl.BlockSpec((8, D), lambda h: (0, 0)),
        ],
        out_specs=[
            pl.BlockSpec((total, 80, D), lambda h: (0, 0, 0)),
            pl.BlockSpec((1, length), lambda h: (0, 0)),
        ],
        out_shape=[
            jax.ShapeDtypeStruct((total, 80, D), BF16),
            jax.ShapeDtypeStruct((1, length), F32),
        ],
        scratch_shapes=[pltpu.VMEM((8, D), F32)],
        compiler_params=pltpu.CompilerParams(vmem_limit_bytes=32 << 20),
        cost_estimate=pl.CostEstimate(
            flops=8 * heads * length * D * D, bytes_accessed=8 * length * width, transcendentals=0
        ),
        name="block_sums",
    )(
        session_start,
        queries,
        key_rows,
        value_rows,
        out_grad,
        cache_states,
        probe_gate.reshape(1, length),
        steer_rows,
    )


def scan_kernel(owner_ref, v_ref, w_ref, steer_ref):
    blocks = v_ref.shape[0]

    def flag_of(b):
        rows = v_ref[b, 64:80, :].astype(F32)[8:16]
        return jnp.concatenate([rows, rows], axis=0) > 0.5

    state = jnp.zeros((PIECE, D), F32)
    steer = jnp.zeros((8, D), F32)
    for b in range(blocks):
        cached = v_ref[owner_ref[b], 48:64, :]
        w_ref[b, 32:48, :] = cached
        w_ref[b, 0:16, :] = state.astype(BF16)
        added = v_ref[b, 0:16, :].astype(F32)
        state = added + jnp.where(flag_of(b), cached.astype(F32), state)
        steer = steer + v_ref[b, 64:80, :].astype(F32)[0:8]
    state = jnp.zeros((PIECE, D), F32)
    for b in reversed(range(blocks)):
        flag = flag_of(b)
        w_ref[b, 16:32, :] = state.astype(BF16)
        begun = (v_ref[b, 32:48, :].astype(F32) + state) * (1.0 / D)
        w_ref[owner_ref[b], 48:64, :] = jnp.where(flag, begun, 0.0).astype(BF16)
        state = v_ref[b, 16:32, :].astype(F32) + jnp.where(flag, 0.0, state)
    tokens = blocks * 1024
    steer_ref[...] = (steer + pltpu.roll(steer, 4, 0)) * (1.0 / math.sqrt(tokens))


def scan_blocks(owner, pieces):
    blocks = pieces.shape[0]
    vmem = pl.BlockSpec(memory_space=pltpu.VMEM)
    return pl.pallas_call(
        scan_kernel,
        in_specs=[pl.BlockSpec(memory_space=pltpu.SMEM), vmem],
        out_specs=[vmem, vmem],
        out_shape=[
            jax.ShapeDtypeStruct((blocks, 64, D), BF16),
            jax.ShapeDtypeStruct((8, D), F32),
        ],
        compiler_params=pltpu.CompilerParams(vmem_limit_bytes=32 << 20),
        name="scan_blocks",
    )(owner, pieces)


def grads_kernel(start_ref, q_ref, k_ref, v_ref, g_ref, w_ref, dq_ref, dk_ref, dv_ref, dc_ref):
    length = q_ref.shape[0]
    start = start_ref[0]
    before, after, final = row_masks(start, length)
    state = w_ref[...]
    enter = state[:, 0:16, :].reshape(D, D)
    leave = state[:, 16:32, :].reshape(D, D)
    cached = state[:, 32:48, :].reshape(D, D)
    dc_ref[0, 0] = state[:, 48:64, :].reshape(D, D)
    enter_cached = jnp.concatenate([enter, cached], axis=1)
    scale = 1.0 / D
    for i in range(length // STRIP):
        lo, hi = i * STRIP, (i + 1) * STRIP
        g = g_ref[lo:hi, :]
        s = lo + lax.broadcasted_iota(jnp.int32, (STRIP, hi), 0)
        t = lax.broadcasted_iota(jnp.int32, (STRIP, hi), 1)
        keep = (t <= s) & (t >= jnp.where(s >= start, start, 0))
        y = jnp.where(keep, nt(g, v_ref[0:hi, :]), 0.0).astype(BF16)
        inter = jnp.concatenate([g * before[lo:hi], g * after[lo:hi]], axis=1)
        dq = nn(y, k_ref[0:hi, :]) + nt(inter, enter_cached)
        dq_ref[lo:hi, :] = (dq * scale).astype(BF16)
    for j in range(length // STRIP):
        lo, hi = j * STRIP, (j + 1) * STRIP
        rest = length - lo
        k = k_ref[lo:hi, :]
        v = v_ref[lo:hi, :]
        t = lo + lax.broadcasted_iota(jnp.int32, (STRIP, rest), 0)
        s = lo + lax.broadcasted_iota(jnp.int32, (STRIP, rest), 1)
        keep = (t <= s) & (s < jnp.where(t < start, start, length))
        yt = jnp.where(keep, nt(v, g_ref[lo:length, :]), 0.0).astype(BF16)
        xt = jnp.where(keep, nt(k, q_ref[lo:length, :]), 0.0).astype(BF16)
        dk = nn(yt, q_ref[lo:length, :]) + nt(v * final[lo:hi], leave)
        dv = nn(xt, g_ref[lo:length, :]) + nn(k * final[lo:hi], leave)
        dk_ref[lo:hi, :] = (dk * scale).astype(BF16)
        dv_ref[lo:hi, :] = (dv * scale).astype(BF16)


def block_grads(queries, key_rows, value_rows, out_grad, session_start, states):
    length, width = queries.shape
    heads = width // D
    pieces = D // PIECE
    column = pl.BlockSpec((length, D), lambda h: (0, h))
    wide = jax.ShapeDtypeStruct((length, width), BF16)
    return pl.pallas_call(
        grads_kernel,
        grid=(heads,),
        in_specs=[
            pl.BlockSpec(memory_space=pltpu.SMEM),
            column,
            column,
            column,
            column,
            pl.BlockSpec((pieces, 64, D), lambda h: (h, 0, 0)),
        ],
        out_specs=[column, column, column, pl.BlockSpec((1, 1, D, D), lambda h: (0, h, 0, 0))],
        out_shape=[wide, wide, wide, jax.ShapeDtypeStruct((1, heads, D, D), BF16)],
        compiler_params=pltpu.CompilerParams(vmem_limit_bytes=48 << 20),
        cost_estimate=pl.CostEstimate(
            flops=10 * heads * length * length * D, bytes_accessed=14 * length * width, transcendentals=0
        ),
        name="block_grads",
    )(session_start, queries, key_rows, value_rows, out_grad, states)


def shards(
    queries,
    key_rows,
    value_rows,
    out_grad,
    cache_states,
    session_start,
    cache_owner,
    probe_gate,
    steer_vector,
):
    heads = steer_vector.shape[0]
    sent, gate = block_sums(
        queries, key_rows, value_rows, out_grad, cache_states, session_start, probe_gate, steer_vector
    )
    pieces = lax.all_to_all(sent, "seq", 0, 0, tiled=True)
    scanned, steer = scan_blocks(cache_owner, pieces)
    states = lax.all_to_all(scanned, "seq", 0, 0, tiled=True)
    grad_queries, grad_keys, grad_values, grad_cache = block_grads(
        queries, key_rows, value_rows, out_grad, session_start, states
    )
    grad_steer = steer[:heads]
    count = lax.axis_size("head")
    step = 1
    while step < count:
        gate = gate + lax.ppermute(gate, "head", [(i, i ^ step) for i in range(count)])
        step *= 2
    return (grad_queries, grad_keys, grad_values, grad_cache, grad_steer, gate.reshape(-1))


def solution(mesh):
    in_specs = (
        P("seq", "head"),
        P("seq", "head"),
        P("seq", "head"),
        P("seq", "head"),
        P("seq", "head", None, None),
        P("seq"),
        P(),
        P("seq"),
        P("head", None),
    )
    out_specs = (
        P("seq", "head"),
        P("seq", "head"),
        P("seq", "head"),
        P("seq", "head", None, None),
        P("head", None),
        P("seq"),
    )
    return jax.shard_map(shards, mesh=mesh, in_specs=in_specs, out_specs=out_specs, check_vma=False)
```

```python
import functools
import math

import jax
import jax.numpy as jnp
from jax import lax
from jax.experimental import pallas as pl
from jax.experimental.pallas import tpu as pltpu
from jax.sharding import PartitionSpec as P

D = 128
PIECE = 16
STRIP = 256
VMEM_BYTES = 63 << 20 | 128 << 10
F32 = jnp.float32
BF16 = jnp.bfloat16


def nt(a, b):
    return lax.dot_general(a, b, (((1,), (1,)), ((), ())), preferred_element_type=F32)


def nn(a, b):
    return lax.dot_general(a, b, (((1,), (0,)), ((), ())), preferred_element_type=F32)


def tn(a, b):
    return lax.dot_general(a, b, (((0,), (0,)), ((), ())), preferred_element_type=F32)


def row_masks(start, length):
    rows = lax.broadcasted_iota(jnp.int32, (length, D), 0)
    after = (rows >= start).astype(F32)
    before = 1.0 - after
    whole = jnp.where(start >= length, 1.0, 0.0).astype(F32)
    final = jnp.maximum(after, whole)
    return before.astype(BF16), after.astype(BF16), final.astype(BF16)


def whole(space):
    return pl.BlockSpec(memory_space=space)


def sums_kernel(
    start_ref, q_any, k_any, v_any, g_any, c_any, probe_ref, steer_ref,
    u_any, gate_ref, q_ref, k_ref, v_ref, g_ref, u_ref, in_sem, c_sem, out_sem,
):
    heads, length, _ = q_ref.shape
    pieces = D // PIECE
    start = start_ref[0]

    def fetches(h):
        pairs = ((k_any, k_ref), (v_any, v_ref), (q_any, q_ref), (g_any, g_ref))
        return [
            pltpu.make_async_copy(far.at[:, h * D : (h + 1) * D], near.at[h], in_sem.at[n, h])
            for n, (far, near) in enumerate(pairs)
        ]

    cached = [
        pltpu.make_async_copy(
            c_any.at[0, h, n * PIECE : (n + 1) * PIECE, :], u_any.at[h * pieces + n, 48:64, :], c_sem.at[h * pieces + n]
        )
        for h in range(heads)
        for n in range(pieces)
    ]
    for h in range(heads):
        for copy in fetches(h):
            copy.start()
    for copy in cached:
        copy.start()

    before, after, final = row_masks(start, length)
    probe = probe_ref[...]
    high = probe.astype(BF16)
    low = (probe - high.astype(F32)).astype(BF16)
    rows = lax.broadcasted_iota(jnp.int32, (8, D), 0)
    flag = jnp.where(start < length, 1.0, 0.0).astype(F32)
    tile = jnp.full((8, D), flag)
    gate = jnp.zeros((heads, length), F32)
    steer = steer_ref[...].astype(F32)
    sent = []
    for h in range(heads):
        for copy in fetches(h):
            copy.wait()
        g = g_ref[h]
        kv = tn(k_ref[h], v_ref[h] * final)
        both = tn(q_ref[h], jnp.concatenate([g * before, g * after], axis=1))
        here = slice(h * pieces, (h + 1) * pieces)
        u_ref[here, 0:16, :] = kv.astype(BF16).reshape(pieces, PIECE, D)
        u_ref[here, 16:32, :] = both[:, :D].astype(BF16).reshape(pieces, PIECE, D)
        u_ref[here, 32:48, :] = both[:, D:].astype(BF16).reshape(pieces, PIECE, D)
        copy = pltpu.make_async_copy(u_ref.at[here, 0:48, :], u_any.at[here, 0:48, :], out_sem.at[h])
        copy.start()
        sent.append(copy)
        steer_sum = nn(high, g) + nn(low, g)
        tile = jnp.where(rows == h, jnp.broadcast_to(steer_sum, (8, D)), tile)
        vector = jnp.where(rows[:heads] == h, steer, 0.0).astype(BF16)
        gate = gate + nt(vector, g)
    gate_ref[...] = jnp.sum(gate, axis=0, keepdims=True)
    u_ref[:, 64:72, :] = jnp.broadcast_to(tile.astype(BF16)[None], (u_ref.shape[0], 8, D))
    copy = pltpu.make_async_copy(u_ref.at[:, 64:72, :], u_any.at[:, 64:72, :], out_sem.at[heads])
    copy.start()
    sent.append(copy)
    for copy in cached + sent:
        copy.wait()


def block_sums(queries, key_rows, value_rows, out_grad, cache_states, session_start, probe_gate, steer_vector):
    length, width = queries.shape
    heads = width // D
    total = heads * D // PIECE
    near = pltpu.VMEM((heads, length, D), BF16)
    hbm, vmem = whole(pltpu.HBM), whole(pltpu.VMEM)
    return pl.pallas_call(
        sums_kernel,
        in_specs=[whole(pltpu.SMEM), hbm, hbm, hbm, hbm, hbm, vmem, vmem],
        out_specs=[hbm, vmem],
        out_shape=[
            jax.ShapeDtypeStruct((total, 72, D), BF16),
            jax.ShapeDtypeStruct((1, length), F32),
        ],
        scratch_shapes=[
            near,
            near,
            near,
            near,
            pltpu.VMEM((total, 72, D), BF16),
            pltpu.SemaphoreType.DMA((4, heads)),
            pltpu.SemaphoreType.DMA((total,)),
            pltpu.SemaphoreType.DMA((heads + 1,)),
        ],
        compiler_params=pltpu.CompilerParams(vmem_limit_bytes=VMEM_BYTES),
        cost_estimate=pl.CostEstimate(
            flops=8 * heads * length * D * D, bytes_accessed=8 * length * width, transcendentals=0
        ),
        name="block_sums",
    )(
        session_start,
        queries,
        key_rows,
        value_rows,
        out_grad,
        cache_states,
        probe_gate.reshape(1, length),
        steer_vector,
    )


def scan_kernel(owner_ref, v_ref, w_ref, steer_ref):
    blocks = v_ref.shape[0]

    def extra(b):
        return v_ref[b, 64:72, :].astype(F32)

    def flag_of(b):
        row = extra(b)[4:5]
        return jnp.broadcast_to(row, (PIECE, D)) > 0.5

    state = jnp.zeros((PIECE, D), F32)
    steer = jnp.zeros((8, D), F32)
    for b in range(blocks):
        cached = v_ref[owner_ref[b], 48:64, :]
        w_ref[b, 32:48, :] = cached
        w_ref[b, 0:16, :] = state.astype(BF16)
        added = v_ref[b, 0:16, :].astype(F32)
        state = added + jnp.where(flag_of(b), cached.astype(F32), state)
        steer = steer + extra(b)
    state = jnp.zeros((PIECE, D), F32)
    for b in reversed(range(blocks)):
        flag = flag_of(b)
        w_ref[b, 16:32, :] = state.astype(BF16)
        begun = (v_ref[b, 32:48, :].astype(F32) + state) * (1.0 / D)
        w_ref[owner_ref[b], 48:64, :] = jnp.where(flag, begun, 0.0).astype(BF16)
        state = v_ref[b, 16:32, :].astype(F32) + jnp.where(flag, 0.0, state)
    tokens = blocks * 1024
    steer_ref[...] = steer[0 : steer_ref.shape[0]] * (1.0 / math.sqrt(tokens))


def scan_blocks(owner, pieces, heads):
    blocks = pieces.shape[0]
    vmem = whole(pltpu.VMEM)
    return pl.pallas_call(
        scan_kernel,
        in_specs=[whole(pltpu.SMEM), vmem],
        out_specs=[vmem, vmem],
        out_shape=[
            jax.ShapeDtypeStruct((blocks, 64, D), BF16),
            jax.ShapeDtypeStruct((heads, D), F32),
        ],
        compiler_params=pltpu.CompilerParams(vmem_limit_bytes=8 << 20),
        name="scan_blocks",
    )(owner, pieces)


def local_kernel(
    start_ref, q_any, k_any, v_any, g_any, pq_any, pk_any, pv_any,
    q_ref, k_ref, v_ref, g_ref, pq_ref, pk_ref, pv_ref, in_sem, out_sem,
):
    heads, length, _ = q_ref.shape
    start = start_ref[0]

    def fetches(h):
        pairs = ((g_any, g_ref), (v_any, v_ref), (k_any, k_ref), (q_any, q_ref))
        columns = pl.ds(pl.multiple_of(h * D, D), D)
        return [
            pltpu.make_async_copy(far.at[:, columns], near.at[h], in_sem.at[n, h])
            for n, (far, near) in enumerate(pairs)
        ]

    def returns(h):
        pairs = ((pq_ref, pq_any), (pk_ref, pk_any), (pv_ref, pv_any))
        return [
            pltpu.make_async_copy(near.at[h], far.at[h], out_sem.at[n, h])
            for n, (near, far) in enumerate(pairs)
        ]

    for h in range(heads):
        for copy in fetches(h):
            copy.start()

    @pl.loop(0, heads)
    def _(h):
        for copy in fetches(h):
            copy.wait()
        for i in range(length // STRIP):
            lo, hi = i * STRIP, (i + 1) * STRIP
            s = lo + lax.broadcasted_iota(jnp.int32, (STRIP, hi), 0)
            t = lax.broadcasted_iota(jnp.int32, (STRIP, hi), 1)
            keep = (t <= s) & (t >= jnp.where(s >= start, start, 0))
            y = jnp.where(keep, nt(g_ref[h, lo:hi, :], v_ref[h, 0:hi, :]), 0.0).astype(BF16)
            pq_ref[h, lo:hi, :] = nn(y, k_ref[h, 0:hi, :])
        for j in range(length // STRIP):
            lo, hi = j * STRIP, (j + 1) * STRIP
            rest = length - lo
            t = lo + lax.broadcasted_iota(jnp.int32, (STRIP, rest), 0)
            s = lo + lax.broadcasted_iota(jnp.int32, (STRIP, rest), 1)
            keep = (t <= s) & (s < jnp.where(t < start, start, length))
            yt = jnp.where(keep, nt(v_ref[h, lo:hi, :], g_ref[h, lo:length, :]), 0.0).astype(BF16)
            pk_ref[h, lo:hi, :] = nn(yt, q_ref[h, lo:length, :])
            xt = jnp.where(keep, nt(k_ref[h, lo:hi, :], q_ref[h, lo:length, :]), 0.0).astype(BF16)
            pv_ref[h, lo:hi, :] = nn(xt, g_ref[h, lo:length, :])
        for copy in returns(h):
            copy.start()

    for h in range(heads):
        for copy in returns(h):
            copy.wait()


def local_grads(session_start, queries, key_rows, value_rows, out_grad):
    length, width = queries.shape
    heads = width // D
    hbm = whole(pltpu.HBM)
    near = pltpu.VMEM((heads, length, D), BF16)
    sums = pltpu.VMEM((heads, length, D), F32)
    part = jax.ShapeDtypeStruct((heads, length, D), F32)
    return pl.pallas_call(
        local_kernel,
        in_specs=[whole(pltpu.SMEM), hbm, hbm, hbm, hbm],
        out_specs=[hbm, hbm, hbm],
        out_shape=[part, part, part],
        scratch_shapes=[near] * 4
        + [sums] * 3
        + [pltpu.SemaphoreType.DMA((4, heads)), pltpu.SemaphoreType.DMA((3, heads))],
        compiler_params=pltpu.CompilerParams(vmem_limit_bytes=VMEM_BYTES),
        cost_estimate=pl.CostEstimate(
            flops=16 * heads * length * length * D, bytes_accessed=20 * heads * length * D, transcendentals=0
        ),
        name="local_grads",
    )(session_start, queries, key_rows, value_rows, out_grad)


def state_kernel(
    start_ref, k_any, v_any, g_any, pq_any, pk_any, pv_any, w_ref,
    dq_any, dk_any, dv_any, dc_any,
    k_ref, v_ref, g_ref, pq_ref, pk_ref, pv_ref, dq_ref, dk_ref, dv_ref, in_sem, c_sem, out_sem,
):
    heads, length, _ = k_ref.shape
    pieces = D // PIECE
    start = start_ref[0]

    def fetches(h):
        columns = slice(h * D, (h + 1) * D)
        pairs = (
            (g_any.at[:, columns], g_ref.at[h]),
            (pq_any.at[h], pq_ref.at[h]),
            (v_any.at[:, columns], v_ref.at[h]),
            (pk_any.at[h], pk_ref.at[h]),
            (k_any.at[:, columns], k_ref.at[h]),
            (pv_any.at[h], pv_ref.at[h]),
        )
        return [pltpu.make_async_copy(far, near, in_sem.at[n, h]) for n, (far, near) in enumerate(pairs)]

    for h in range(heads):
        for copy in fetches(h):
            copy.start()
    copies = [
        pltpu.make_async_copy(
            w_ref.at[h * pieces + n, 48:64, :], dc_any.at[0, h, n * PIECE : (n + 1) * PIECE, :], c_sem.at[h * pieces + n]
        )
        for h in range(heads)
        for n in range(pieces)
    ]
    for copy in copies:
        copy.start()
    before, after, final = row_masks(start, length)
    scale = 1.0 / D
    for h in range(heads):
        for copy in fetches(h):
            copy.wait()
        here = slice(h * pieces, (h + 1) * pieces)
        enter = w_ref[here, 0:16, :].reshape(D, D)
        leave = w_ref[here, 16:32, :].reshape(D, D)
        cached = w_ref[here, 32:48, :].reshape(D, D)
        g = g_ref[h]
        inter = jnp.concatenate([g * before, g * after], axis=1)
        dq = pq_ref[h] + nt(inter, jnp.concatenate([enter, cached], axis=1))
        dq_ref[h] = (dq * scale).astype(BF16)
        dk = pk_ref[h] + nt(v_ref[h] * final, leave)
        dk_ref[h] = (dk * scale).astype(BF16)
        dv = pv_ref[h] + nn(k_ref[h] * final, leave)
        dv_ref[h] = (dv * scale).astype(BF16)
        for n, (near, far) in enumerate(((dq_ref, dq_any), (dk_ref, dk_any), (dv_ref, dv_any))):
            copy = pltpu.make_async_copy(near.at[h], far.at[:, h * D : (h + 1) * D], out_sem.at[n, h])
            copy.start()
            copies.append(copy)
    for copy in copies:
        copy.wait()


def state_grads(session_start, key_rows, value_rows, out_grad, parts, states):
    heads, length, _ = parts[0].shape
    total = heads * D // PIECE
    hbm = whole(pltpu.HBM)
    near = pltpu.VMEM((heads, length, D), BF16)
    sums = pltpu.VMEM((heads, length, D), F32)
    wide = jax.ShapeDtypeStruct((length, heads * D), BF16)
    return pl.pallas_call(
        state_kernel,
        in_specs=[whole(pltpu.SMEM)] + [hbm] * 6 + [whole(pltpu.VMEM)],
        out_specs=[hbm] * 4,
        out_shape=[wide, wide, wide, jax.ShapeDtypeStruct((1, heads, D, D), BF16)],
        scratch_shapes=[
            near,
            near,
            near,
            sums,
            sums,
            sums,
            near,
            near,
            near,
            pltpu.SemaphoreType.DMA((6, heads)),
            pltpu.SemaphoreType.DMA((total,)),
            pltpu.SemaphoreType.DMA((3, heads)),
        ],
        compiler_params=pltpu.CompilerParams(vmem_limit_bytes=VMEM_BYTES),
        cost_estimate=pl.CostEstimate(
            flops=8 * heads * length * D * D, bytes_accessed=20 * heads * length * D, transcendentals=0
        ),
        name="state_grads",
    )(session_start, key_rows, value_rows, out_grad, *parts, states)


def shards(
    queries,
    key_rows,
    value_rows,
    out_grad,
    cache_states,
    session_start,
    cache_owner,
    probe_gate,
    steer_vector,
):
    heads = steer_vector.shape[0]
    sent, gate = block_sums(
        queries, key_rows, value_rows, out_grad, cache_states, session_start, probe_gate, steer_vector
    )
    pieces = lax.all_to_all(sent, "seq", 0, 0, tiled=True)
    parts = local_grads(session_start, queries, key_rows, value_rows, out_grad)
    pieces, parts = lax.optimization_barrier((pieces, parts))
    scanned, grad_steer = scan_blocks(cache_owner, pieces, heads)
    states = lax.all_to_all(scanned, "seq", 0, 0, tiled=True)
    grad_queries, grad_keys, grad_values, grad_cache = state_grads(
        session_start, key_rows, value_rows, out_grad, parts, states
    )
    count = lax.axis_size("head")
    step = 1
    while step < count:
        gate = gate + lax.ppermute(gate, "head", [(i, i ^ step) for i in range(count)])
        step *= 2
    return (grad_queries, grad_keys, grad_values, grad_cache, grad_steer, gate.reshape(-1))


def solution(mesh):
    in_specs = (
        P("seq", "head"),
        P("seq", "head"),
        P("seq", "head"),
        P("seq", "head"),
        P("seq", "head", None, None),
        P("seq"),
        P(),
        P("seq"),
        P("head", None),
    )
    out_specs = (
        P("seq", "head"),
        P("seq", "head"),
        P("seq", "head"),
        P("seq", "head", None, None),
        P("head", None),
        P("seq"),
    )
    return jax.shard_map(shards, mesh=mesh, in_specs=in_specs, out_specs=out_specs, check_vma=False)
```

```python
import functools
import math

import jax
import jax.numpy as jnp
from jax import lax
from jax.experimental import pallas as pl
from jax.experimental.pallas import tpu as pltpu
from jax.sharding import PartitionSpec as P

D = 128
PIECE = 16
STRIP = 256
VMEM_BYTES = 61 << 20
STATE_BYTES = 48 << 20
AHEAD = 2
F32 = jnp.float32
BF16 = jnp.bfloat16


def nt(a, b):
    return lax.dot_general(a, b, (((1,), (1,)), ((), ())), preferred_element_type=F32)


def nn(a, b):
    return lax.dot_general(a, b, (((1,), (0,)), ((), ())), preferred_element_type=F32)


def tn(a, b):
    return lax.dot_general(a, b, (((0,), (0,)), ((), ())), preferred_element_type=F32)


def row_masks(start, length):
    rows = lax.broadcasted_iota(jnp.int32, (length, D), 0)
    after = (rows >= start).astype(F32)
    before = 1.0 - after
    whole = jnp.where(start >= length, 1.0, 0.0).astype(F32)
    final = jnp.maximum(after, whole)
    return before.astype(BF16), after.astype(BF16), final.astype(BF16)


def whole(space):
    return pl.BlockSpec(memory_space=space)


def sums_kernel(
    start_ref, q_any, k_any, v_any, g_any, c_any, probe_ref, steer_ref,
    u_any, gate_ref, q_ref, k_ref, v_ref, g_ref, u_ref, in_sem, c_sem, out_sem,
):
    heads, length, _ = q_ref.shape
    pieces = D // PIECE
    start = start_ref[0]

    def fetches(h):
        pairs = ((k_any, k_ref), (v_any, v_ref), (q_any, q_ref), (g_any, g_ref))
        return [
            pltpu.make_async_copy(far.at[:, h * D : (h + 1) * D], near.at[h], in_sem.at[n, h])
            for n, (far, near) in enumerate(pairs)
        ]

    for h in range(AHEAD):
        for copy in fetches(h):
            copy.start()
    cached = pltpu.make_async_copy(c_any, u_any.at[:, 48:64, :], c_sem)
    cached.start()

    before, after, final = row_masks(start, length)
    probe = probe_ref[...]
    high = probe.astype(BF16)
    low = (probe - high.astype(F32)).astype(BF16)
    rows = lax.broadcasted_iota(jnp.int32, (8, D), 0)
    flag = jnp.where(start < length, 1.0, 0.0).astype(F32)
    tile = jnp.full((8, D), flag)
    gate = jnp.zeros((heads, length), F32)
    steer = steer_ref[...].astype(F32)
    sent = []
    for h in range(heads):
        for copy in fetches(h):
            copy.wait()
        if h + AHEAD < heads:
            for copy in fetches(h + AHEAD):
                copy.start()
        g = g_ref[h]
        kv = tn(k_ref[h], v_ref[h] * final)
        both = tn(q_ref[h], jnp.concatenate([g * before, g * after], axis=1))
        here = slice(h * pieces, (h + 1) * pieces)
        u_ref[here, 0:16, :] = kv.astype(BF16).reshape(pieces, PIECE, D)
        u_ref[here, 16:32, :] = both[:, :D].astype(BF16).reshape(pieces, PIECE, D)
        u_ref[here, 32:48, :] = both[:, D:].astype(BF16).reshape(pieces, PIECE, D)
        copy = pltpu.make_async_copy(u_ref.at[here, 0:48, :], u_any.at[here, 0:48, :], out_sem.at[h])
        copy.start()
        sent.append(copy)
        steer_sum = nn(high, g) + nn(low, g)
        tile = jnp.where(rows == h, jnp.broadcast_to(steer_sum, (8, D)), tile)
        vector = jnp.where(rows[:heads] == h, steer, 0.0).astype(BF16)
        gate = gate + nt(vector, g)
    gate_ref[...] = jnp.sum(gate, axis=0, keepdims=True)
    u_ref[:, 64:72, :] = jnp.broadcast_to(tile.astype(BF16)[None], (u_ref.shape[0], 8, D))
    copy = pltpu.make_async_copy(u_ref.at[:, 64:72, :], u_any.at[:, 64:72, :], out_sem.at[heads])
    copy.start()
    sent.append(copy)
    for copy in [cached] + sent:
        copy.wait()


def block_sums(queries, key_rows, value_rows, out_grad, cache_states, session_start, probe_gate, steer_vector):
    length, width = queries.shape
    heads = width // D
    total = heads * D // PIECE
    near = pltpu.VMEM((heads, length, D), BF16)
    hbm, vmem = whole(pltpu.HBM), whole(pltpu.VMEM)
    return pl.pallas_call(
        sums_kernel,
        in_specs=[whole(pltpu.SMEM), hbm, hbm, hbm, hbm, hbm, vmem, vmem],
        out_specs=[hbm, vmem],
        out_shape=[
            jax.ShapeDtypeStruct((total, 72, D), BF16),
            jax.ShapeDtypeStruct((1, length), F32),
        ],
        scratch_shapes=[
            near,
            near,
            near,
            near,
            pltpu.VMEM((total, 72, D), BF16),
            pltpu.SemaphoreType.DMA((4, heads)),
            pltpu.SemaphoreType.DMA(()),
            pltpu.SemaphoreType.DMA((heads + 1,)),
        ],
        compiler_params=pltpu.CompilerParams(vmem_limit_bytes=VMEM_BYTES),
        cost_estimate=pl.CostEstimate(
            flops=8 * heads * length * D * D, bytes_accessed=8 * length * width, transcendentals=0
        ),
        name="block_sums",
    )(
        session_start,
        queries,
        key_rows,
        value_rows,
        out_grad,
        cache_states.reshape(total, PIECE, D),
        probe_gate.reshape(1, length),
        steer_vector,
    )


def scan_kernel(owner_ref, v_ref, w_any, steer_ref, w_ref, sem):
    blocks = v_ref.shape[0]

    def extra(b):
        return v_ref[b, 64:72, :].astype(F32)

    def flag_of(b):
        row = extra(b)[4:5]
        return jnp.broadcast_to(row, (PIECE, D)) > 0.5

    state = jnp.zeros((PIECE, D), F32)
    steer = jnp.zeros((8, D), F32)
    for b in range(blocks):
        cached = v_ref[owner_ref[b], 48:64, :]
        w_ref[b, 0:16, :] = state.astype(BF16)
        w_ref[b, 16:32, :] = cached
        added = v_ref[b, 0:16, :].astype(F32)
        state = added + jnp.where(flag_of(b), cached.astype(F32), state)
        steer = steer + extra(b)
    first = pltpu.make_async_copy(w_ref.at[:, 0:32, :], w_any.at[:, 0:32, :], sem.at[0])
    first.start()
    state = jnp.zeros((PIECE, D), F32)
    for b in reversed(range(blocks)):
        flag = flag_of(b)
        w_ref[b, 32:48, :] = state.astype(BF16)
        begun = (v_ref[b, 32:48, :].astype(F32) + state) * (1.0 / D)
        w_ref[owner_ref[b], 48:64, :] = jnp.where(flag, begun, 0.0).astype(BF16)
        state = v_ref[b, 16:32, :].astype(F32) + jnp.where(flag, 0.0, state)
    second = pltpu.make_async_copy(w_ref.at[:, 32:64, :], w_any.at[:, 32:64, :], sem.at[1])
    second.start()
    tokens = blocks * 1024
    steer_ref[...] = steer[0 : steer_ref.shape[0]] * (1.0 / math.sqrt(tokens))
    first.wait()
    second.wait()


def scan_blocks(owner, pieces, heads):
    blocks = pieces.shape[0]
    hbm, vmem = whole(pltpu.HBM), whole(pltpu.VMEM)
    return pl.pallas_call(
        scan_kernel,
        in_specs=[whole(pltpu.SMEM), vmem],
        out_specs=[hbm, vmem],
        out_shape=[
            jax.ShapeDtypeStruct((blocks, 64, D), BF16),
            jax.ShapeDtypeStruct((heads, D), F32),
        ],
        scratch_shapes=[pltpu.VMEM((blocks, 64, D), BF16), pltpu.SemaphoreType.DMA((2,))],
        compiler_params=pltpu.CompilerParams(vmem_limit_bytes=VMEM_BYTES),
        name="scan_blocks",
    )(owner, pieces)


def local_kernel(
    start_ref, q_any, k_any, v_any, g_any, part_any, q_ref, k_ref, v_ref, g_ref, part_ref, in_sem, out_sem
):
    heads, length, _ = q_ref.shape
    start = start_ref[0]

    def fetches(h):
        pairs = ((g_any, g_ref), (v_any, v_ref), (k_any, k_ref), (q_any, q_ref))
        columns = pl.ds(pl.multiple_of(h * D, D), D)
        return [
            pltpu.make_async_copy(far.at[:, columns], near.at[h], in_sem.at[n, h])
            for n, (far, near) in enumerate(pairs)
        ]

    def result(h):
        return pltpu.make_async_copy(part_ref.at[:, h], part_any.at[:, h], out_sem.at[h])

    for h in range(AHEAD):
        for copy in fetches(h):
            copy.start()

    @pl.loop(0, heads)
    def _(h):
        for copy in fetches(h):
            copy.wait()

        @pl.when(h + AHEAD < heads)
        def _():
            for copy in fetches(h + AHEAD):
                copy.start()

        for i in range(length // STRIP):
            lo, hi = i * STRIP, (i + 1) * STRIP
            s = lo + lax.broadcasted_iota(jnp.int32, (STRIP, hi), 0)
            t = lax.broadcasted_iota(jnp.int32, (STRIP, hi), 1)
            keep = (t <= s) & (t >= jnp.where(s >= start, start, 0))
            y = jnp.where(keep, nt(g_ref[h, lo:hi, :], v_ref[h, 0:hi, :]), 0.0).astype(BF16)
            part_ref[0, h, lo:hi, :] = nn(y, k_ref[h, 0:hi, :]).astype(BF16)
        for j in range(length // STRIP):
            lo, hi = j * STRIP, (j + 1) * STRIP
            rest = length - lo
            t = lo + lax.broadcasted_iota(jnp.int32, (STRIP, rest), 0)
            s = lo + lax.broadcasted_iota(jnp.int32, (STRIP, rest), 1)
            keep = (t <= s) & (s < jnp.where(t < start, start, length))
            yt = jnp.where(keep, nt(v_ref[h, lo:hi, :], g_ref[h, lo:length, :]), 0.0).astype(BF16)
            part_ref[1, h, lo:hi, :] = nn(yt, q_ref[h, lo:length, :]).astype(BF16)
            xt = jnp.where(keep, nt(k_ref[h, lo:hi, :], q_ref[h, lo:length, :]), 0.0).astype(BF16)
            part_ref[2, h, lo:hi, :] = nn(xt, g_ref[h, lo:length, :]).astype(BF16)
        result(h).start()

    for h in range(heads):
        result(h).wait()


def local_grads(session_start, queries, key_rows, value_rows, out_grad):
    length, width = queries.shape
    heads = width // D
    hbm = whole(pltpu.HBM)
    near = pltpu.VMEM((heads, length, D), BF16)
    return pl.pallas_call(
        local_kernel,
        in_specs=[whole(pltpu.SMEM), hbm, hbm, hbm, hbm],
        out_specs=hbm,
        out_shape=jax.ShapeDtypeStruct((3, heads, length, D), BF16),
        scratch_shapes=[near] * 4
        + [
            pltpu.VMEM((3, heads, length, D), BF16),
            pltpu.SemaphoreType.DMA((4, heads)),
            pltpu.SemaphoreType.DMA((heads,)),
        ],
        compiler_params=pltpu.CompilerParams(vmem_limit_bytes=VMEM_BYTES),
        cost_estimate=pl.CostEstimate(
            flops=16 * heads * length * length * D, bytes_accessed=20 * heads * length * D, transcendentals=0
        ),
        name="local_grads",
    )(session_start, queries, key_rows, value_rows, out_grad)


def state_kernel(
    start_ref, k_ref, v_ref, g_ref, part_any, w_ref,
    dq_any, dk_any, dv_any, dc_any, part_ref, out_ref, in_sem, c_sem, out_sem,
):
    _, heads, length, _ = part_ref.shape
    pieces = D // PIECE
    start = start_ref[0]

    def fetch(h):
        return pltpu.make_async_copy(part_any.at[:, h], part_ref.at[:, h], in_sem.at[h])

    for h in range(heads):
        fetch(h).start()
    copies = [pltpu.make_async_copy(w_ref.at[:, 48:64, :], dc_any, c_sem)]
    copies[0].start()
    before, after, final = row_masks(start, length)
    scale = 1.0 / D
    for h in range(heads):
        fetch(h).wait()
        columns = slice(h * D, (h + 1) * D)
        here = slice(h * pieces, (h + 1) * pieces)
        enter = w_ref[here, 0:16, :].reshape(D, D)
        cached = w_ref[here, 16:32, :].reshape(D, D)
        leave = w_ref[here, 32:48, :].reshape(D, D)
        g = g_ref[:, columns]
        inter = jnp.concatenate([g * before, g * after], axis=1)
        dq = part_ref[0, h].astype(F32) + nt(inter, jnp.concatenate([enter, cached], axis=1))
        out_ref[0, h] = (dq * scale).astype(BF16)
        dk = part_ref[1, h].astype(F32) + nt(v_ref[:, columns] * final, leave)
        out_ref[1, h] = (dk * scale).astype(BF16)
        dv = part_ref[2, h].astype(F32) + nn(k_ref[:, columns] * final, leave)
        out_ref[2, h] = (dv * scale).astype(BF16)
        for n, far in enumerate((dq_any, dk_any, dv_any)):
            copy = pltpu.make_async_copy(out_ref.at[n, h], far.at[:, columns], out_sem.at[n, h])
            copy.start()
            copies.append(copy)
    for copy in copies:
        copy.wait()


def state_grads(session_start, key_rows, value_rows, out_grad, parts, states):
    _, heads, length, _ = parts.shape
    total = heads * D // PIECE
    hbm, vmem = whole(pltpu.HBM), whole(pltpu.VMEM)
    near = pltpu.VMEM((3, heads, length, D), BF16)
    wide = jax.ShapeDtypeStruct((length, heads * D), BF16)
    *grads, grad_cache = pl.pallas_call(
        state_kernel,
        in_specs=[whole(pltpu.SMEM), vmem, vmem, vmem, hbm, vmem],
        out_specs=[hbm] * 4,
        out_shape=[wide, wide, wide, jax.ShapeDtypeStruct((total, PIECE, D), BF16)],
        scratch_shapes=[
            near,
            near,
            pltpu.SemaphoreType.DMA((heads,)),
            pltpu.SemaphoreType.DMA(()),
            pltpu.SemaphoreType.DMA((3, heads)),
        ],
        compiler_params=pltpu.CompilerParams(vmem_limit_bytes=STATE_BYTES),
        cost_estimate=pl.CostEstimate(
            flops=8 * heads * length * D * D, bytes_accessed=20 * heads * length * D, transcendentals=0
        ),
        name="state_grads",
    )(session_start, key_rows, value_rows, out_grad, parts, states)
    return *grads, grad_cache.reshape(1, heads, D, D)


def shards(
    queries,
    key_rows,
    value_rows,
    out_grad,
    cache_states,
    session_start,
    cache_owner,
    probe_gate,
    steer_vector,
):
    heads = steer_vector.shape[0]
    sent, gate = block_sums(
        queries, key_rows, value_rows, out_grad, cache_states, session_start, probe_gate, steer_vector
    )
    pieces = lax.all_to_all(sent, "seq", 0, 0, tiled=True)
    parts = local_grads(session_start, queries, key_rows, value_rows, out_grad)
    pieces, parts = lax.optimization_barrier((pieces, parts))
    scanned, grad_steer = scan_blocks(cache_owner, pieces, heads)
    states = lax.all_to_all(scanned, "seq", 0, 0, tiled=True)
    grad_queries, grad_keys, grad_values, grad_cache = state_grads(
        session_start, key_rows, value_rows, out_grad, parts, states
    )
    count = lax.axis_size("head")
    step = 1
    while step < count:
        gate = gate + lax.ppermute(gate, "head", [(i, i ^ step) for i in range(count)])
        step *= 2
    return (grad_queries, grad_keys, grad_values, grad_cache, grad_steer, gate.reshape(-1))


def solution(mesh):
    in_specs = (
        P("seq", "head"),
        P("seq", "head"),
        P("seq", "head"),
        P("seq", "head"),
        P("seq", "head", None, None),
        P("seq"),
        P(),
        P("seq"),
        P("head", None),
    )
    out_specs = (
        P("seq", "head"),
        P("seq", "head"),
        P("seq", "head"),
        P("seq", "head", None, None),
        P("head", None),
        P("seq"),
    )
    return jax.shard_map(shards, mesh=mesh, in_specs=in_specs, out_specs=out_specs, check_vma=False)
```

```python
import functools
import math

import jax
import jax.numpy as jnp
from jax import lax
from jax.experimental import pallas as pl
from jax.experimental.pallas import tpu as pltpu
from jax.sharding import PartitionSpec as P

D = 128
PIECE = 16
STRIP = 256
VMEM_BYTES = 60 << 20
STATE_BYTES = 48 << 20
AHEAD = 2
F32 = jnp.float32
BF16 = jnp.bfloat16


def nt(a, b):
    return lax.dot_general(a, b, (((1,), (1,)), ((), ())), preferred_element_type=F32)


def nn(a, b):
    return lax.dot_general(a, b, (((1,), (0,)), ((), ())), preferred_element_type=F32)


def tn(a, b):
    return lax.dot_general(a, b, (((0,), (0,)), ((), ())), preferred_element_type=F32)


def row_masks(start, length):
    rows = lax.broadcasted_iota(jnp.int32, (length, D), 0)
    after = (rows >= start).astype(F32)
    before = 1.0 - after
    whole = jnp.where(start >= length, 1.0, 0.0).astype(F32)
    final = jnp.maximum(after, whole)
    return before.astype(BF16), after.astype(BF16), final.astype(BF16)


def whole(space):
    return pl.BlockSpec(memory_space=space)


def sums_kernel(
    start_any, q_any, k_any, v_any, g_any, c_any, probe_any, steer_any, u_any, gate_ref,
    start_ref, q_ref, k_ref, v_ref, g_ref, probe_ref, steer_ref, u_ref, in_sem, few_sem, out_sem,
):
    heads, length, _ = q_ref.shape
    pieces = D // PIECE

    def fetches(h):
        pairs = ((k_any, k_ref), (v_any, v_ref), (q_any, q_ref), (g_any, g_ref))
        return [
            pltpu.make_async_copy(far.at[:, h * D : (h + 1) * D], near.at[h], in_sem.at[n, h])
            for n, (far, near) in enumerate(pairs)
        ]

    few = [
        pltpu.make_async_copy(start_any, start_ref, few_sem.at[0]),
        pltpu.make_async_copy(probe_any, probe_ref, few_sem.at[1]),
        pltpu.make_async_copy(steer_any, steer_ref, few_sem.at[2]),
        pltpu.make_async_copy(c_any, u_ref.at[:, 48:64, :], few_sem.at[3]),
    ]
    few[0].start()
    for h in range(AHEAD):
        for copy in fetches(h):
            copy.start()
    for copy in few[1:]:
        copy.start()
    few[0].wait()
    start = start_ref[0]
    before, after, final = row_masks(start, length)
    for copy in few[1:]:
        copy.wait()
    probe = probe_ref[...]
    high = probe.astype(BF16)
    low = (probe - high.astype(F32)).astype(BF16)
    steer = steer_ref[...].astype(F32)
    rows = lax.broadcasted_iota(jnp.int32, (8, D), 0)
    flag = jnp.where(start < length, 1.0, 0.0).astype(F32)
    tile = jnp.full((8, D), flag)
    gate = jnp.zeros((heads, length), F32)
    sent = []
    for h in range(heads):
        for copy in fetches(h):
            copy.wait()
        if h + AHEAD < heads:
            for copy in fetches(h + AHEAD):
                copy.start()
        g = g_ref[h]
        kv = tn(k_ref[h], v_ref[h] * final)
        both = tn(q_ref[h], jnp.concatenate([g * before, g * after], axis=1))
        here = slice(h * pieces, (h + 1) * pieces)
        u_ref[here, 0:16, :] = kv.astype(BF16).reshape(pieces, PIECE, D)
        u_ref[here, 16:32, :] = both[:, :D].astype(BF16).reshape(pieces, PIECE, D)
        u_ref[here, 32:48, :] = both[:, D:].astype(BF16).reshape(pieces, PIECE, D)
        copy = pltpu.make_async_copy(u_ref.at[here, 0:64, :], u_any.at[here, 0:64, :], out_sem.at[h])
        copy.start()
        sent.append(copy)
        steer_sum = nn(high, g) + nn(low, g)
        tile = jnp.where(rows == h, jnp.broadcast_to(steer_sum, (8, D)), tile)
        vector = jnp.where(rows[:heads] == h, steer, 0.0).astype(BF16)
        gate = gate + nt(vector, g)
    u_ref[:, 64:72, :] = jnp.broadcast_to(tile.astype(BF16)[None], (u_ref.shape[0], 8, D))
    copy = pltpu.make_async_copy(u_ref.at[:, 64:72, :], u_any.at[:, 64:72, :], out_sem.at[heads])
    copy.start()
    sent.append(copy)
    gate_ref[...] = jnp.sum(gate, axis=0, keepdims=True)
    for copy in sent:
        copy.wait()


def block_sums(queries, key_rows, value_rows, out_grad, cache_states, session_start, probe_gate, steer_vector):
    length, width = queries.shape
    heads = width // D
    total = heads * D // PIECE
    near = pltpu.VMEM((heads, length, D), BF16)
    hbm, vmem = whole(pltpu.HBM), whole(pltpu.VMEM)
    return pl.pallas_call(
        sums_kernel,
        in_specs=[hbm] * 8,
        out_specs=[hbm, vmem],
        out_shape=[
            jax.ShapeDtypeStruct((total, 72, D), BF16),
            jax.ShapeDtypeStruct((1, length), F32),
        ],
        scratch_shapes=[
            pltpu.SMEM(session_start.shape, jnp.int32),
            near,
            near,
            near,
            near,
            pltpu.VMEM((1, length), F32),
            pltpu.VMEM(steer_vector.shape, BF16),
            pltpu.VMEM((total, 72, D), BF16),
            pltpu.SemaphoreType.DMA((4, heads)),
            pltpu.SemaphoreType.DMA((4,)),
            pltpu.SemaphoreType.DMA((heads + 1,)),
        ],
        compiler_params=pltpu.CompilerParams(vmem_limit_bytes=VMEM_BYTES),
        cost_estimate=pl.CostEstimate(
            flops=8 * heads * length * D * D, bytes_accessed=8 * length * width, transcendentals=0
        ),
        name="block_sums",
    )(
        session_start,
        queries,
        key_rows,
        value_rows,
        out_grad,
        cache_states.reshape(total, PIECE, D),
        probe_gate.reshape(1, length),
        steer_vector,
    )


def scan_kernel(owner_any, v_any, w_any, steer_ref, owner_ref, v_ref, w_ref, in_sem, out_sem):
    blocks = v_ref.shape[0]
    fetched = [pltpu.make_async_copy(owner_any, owner_ref, in_sem.at[0])]
    for n, rows in enumerate((slice(48, 72), slice(0, 16), slice(16, 48))):
        fetched.append(pltpu.make_async_copy(v_any.at[:, rows, :], v_ref.at[:, rows, :], in_sem.at[n + 1]))
    for copy in fetched:
        copy.start()

    def extra(b):
        return v_ref[b, 64:72, :].astype(F32)

    def flag_of(b):
        row = extra(b)[4:5]
        return jnp.broadcast_to(row, (PIECE, D)) > 0.5

    state = jnp.zeros((PIECE, D), F32)
    steer = jnp.zeros((8, D), F32)
    for copy in fetched[:3]:
        copy.wait()
    for b in range(blocks):
        cached = v_ref[owner_ref[b], 48:64, :]
        w_ref[b, 0:16, :] = state.astype(BF16)
        w_ref[b, 16:32, :] = cached
        added = v_ref[b, 0:16, :].astype(F32)
        state = added + jnp.where(flag_of(b), cached.astype(F32), state)
        steer = steer + extra(b)
    first = pltpu.make_async_copy(w_ref.at[:, 0:32, :], w_any.at[:, 0:32, :], out_sem.at[0])
    first.start()
    fetched[3].wait()
    state = jnp.zeros((PIECE, D), F32)
    for b in reversed(range(blocks)):
        flag = flag_of(b)
        w_ref[b, 32:48, :] = state.astype(BF16)
        begun = (v_ref[b, 32:48, :].astype(F32) + state) * (1.0 / D)
        w_ref[owner_ref[b], 48:64, :] = jnp.where(flag, begun, 0.0).astype(BF16)
        state = v_ref[b, 16:32, :].astype(F32) + jnp.where(flag, 0.0, state)
    second = pltpu.make_async_copy(w_ref.at[:, 32:64, :], w_any.at[:, 32:64, :], out_sem.at[1])
    second.start()
    tokens = blocks * 1024
    steer_ref[...] = steer[0 : steer_ref.shape[0]] * (1.0 / math.sqrt(tokens))
    first.wait()
    second.wait()


def scan_blocks(owner, pieces, heads):
    blocks = pieces.shape[0]
    hbm, vmem = whole(pltpu.HBM), whole(pltpu.VMEM)
    return pl.pallas_call(
        scan_kernel,
        in_specs=[hbm, hbm],
        out_specs=[hbm, vmem],
        out_shape=[
            jax.ShapeDtypeStruct((blocks, 64, D), BF16),
            jax.ShapeDtypeStruct((heads, D), F32),
        ],
        scratch_shapes=[
            pltpu.SMEM(owner.shape, jnp.int32),
            pltpu.VMEM(pieces.shape, BF16),
            pltpu.VMEM((blocks, 64, D), BF16),
            pltpu.SemaphoreType.DMA((4,)),
            pltpu.SemaphoreType.DMA((2,)),
        ],
        compiler_params=pltpu.CompilerParams(vmem_limit_bytes=VMEM_BYTES),
        name="scan_blocks",
    )(owner, pieces)


def local_kernel(
    start_any, q_any, k_any, v_any, g_any, part_any,
    start_ref, q_ref, k_ref, v_ref, g_ref, part_ref, start_sem, in_sem, out_sem,
):
    heads, length, _ = q_ref.shape
    started = pltpu.make_async_copy(start_any, start_ref, start_sem)
    started.start()

    def fetches(h):
        pairs = ((g_any, g_ref), (v_any, v_ref), (k_any, k_ref), (q_any, q_ref))
        columns = pl.ds(pl.multiple_of(h * D, D), D)
        return [
            pltpu.make_async_copy(far.at[:, columns], near.at[h], in_sem.at[n, h])
            for n, (far, near) in enumerate(pairs)
        ]

    def result(h):
        return pltpu.make_async_copy(part_ref.at[:, h], part_any.at[:, h], out_sem.at[h])

    for h in range(AHEAD):
        for copy in fetches(h):
            copy.start()

    started.wait()
    start = start_ref[0]

    @pl.loop(0, heads)
    def _(h):
        for copy in fetches(h):
            copy.wait()

        @pl.when(h + AHEAD < heads)
        def _():
            for copy in fetches(h + AHEAD):
                copy.start()

        for i in range(length // STRIP):
            lo, hi = i * STRIP, (i + 1) * STRIP
            s = lo + lax.broadcasted_iota(jnp.int32, (STRIP, hi), 0)
            t = lax.broadcasted_iota(jnp.int32, (STRIP, hi), 1)
            keep = (t <= s) & (t >= jnp.where(s >= start, start, 0))
            y = jnp.where(keep, nt(g_ref[h, lo:hi, :], v_ref[h, 0:hi, :]), 0.0).astype(BF16)
            part_ref[0, h, lo:hi, :] = nn(y, k_ref[h, 0:hi, :]).astype(BF16)
        for j in range(length // STRIP):
            lo, hi = j * STRIP, (j + 1) * STRIP
            rest = length - lo
            t = lo + lax.broadcasted_iota(jnp.int32, (STRIP, rest), 0)
            s = lo + lax.broadcasted_iota(jnp.int32, (STRIP, rest), 1)
            keep = (t <= s) & (s < jnp.where(t < start, start, length))
            yt = jnp.where(keep, nt(v_ref[h, lo:hi, :], g_ref[h, lo:length, :]), 0.0).astype(BF16)
            part_ref[1, h, lo:hi, :] = nn(yt, q_ref[h, lo:length, :]).astype(BF16)
            xt = jnp.where(keep, nt(k_ref[h, lo:hi, :], q_ref[h, lo:length, :]), 0.0).astype(BF16)
            part_ref[2, h, lo:hi, :] = nn(xt, g_ref[h, lo:length, :]).astype(BF16)
        result(h).start()

    for h in range(heads):
        result(h).wait()


def local_grads(session_start, queries, key_rows, value_rows, out_grad):
    length, width = queries.shape
    heads = width // D
    hbm = whole(pltpu.HBM)
    near = pltpu.VMEM((heads, length, D), BF16)
    return pl.pallas_call(
        local_kernel,
        in_specs=[hbm] * 5,
        out_specs=hbm,
        out_shape=jax.ShapeDtypeStruct((3, heads, length, D), BF16),
        scratch_shapes=[pltpu.SMEM(session_start.shape, jnp.int32)]
        + [near] * 4
        + [
            pltpu.VMEM((3, heads, length, D), BF16),
            pltpu.SemaphoreType.DMA(()),
            pltpu.SemaphoreType.DMA((4, heads)),
            pltpu.SemaphoreType.DMA((heads,)),
        ],
        compiler_params=pltpu.CompilerParams(vmem_limit_bytes=VMEM_BYTES),
        cost_estimate=pl.CostEstimate(
            flops=16 * heads * length * length * D, bytes_accessed=20 * heads * length * D, transcendentals=0
        ),
        name="local_grads",
    )(session_start, queries, key_rows, value_rows, out_grad)


def state_kernel(
    start_any, k_ref, v_ref, g_ref, part_any, w_any,
    dq_any, dk_any, dv_any, dc_any,
    start_ref, part_ref, w_ref, out_ref, start_sem, in_sem, w_sem, c_sem, out_sem,
):
    _, heads, length, _ = part_ref.shape
    pieces = D // PIECE

    def fetch(h):
        return pltpu.make_async_copy(part_any.at[:, h], part_ref.at[:, h], in_sem.at[h])

    def states(h):
        here = slice(h * pieces, (h + 1) * pieces)
        return pltpu.make_async_copy(w_any.at[here], w_ref.at[here], w_sem.at[h])

    def cache(h):
        here = slice(h * pieces, (h + 1) * pieces)
        return pltpu.make_async_copy(w_ref.at[here, 48:64, :], dc_any.at[here], c_sem.at[h])

    started = pltpu.make_async_copy(start_any, start_ref, start_sem)
    started.start()
    for h in range(heads):
        states(h).start()
        fetch(h).start()
    copies = []
    started.wait()
    start = start_ref[0]
    before, after, final = row_masks(start, length)
    scale = 1.0 / D
    for h in range(heads):
        fetch(h).wait()
        states(h).wait()
        cache(h).start()
        copies.append(cache(h))
        columns = slice(h * D, (h + 1) * D)
        here = slice(h * pieces, (h + 1) * pieces)
        enter = w_ref[here, 0:16, :].reshape(D, D)
        cached = w_ref[here, 16:32, :].reshape(D, D)
        leave = w_ref[here, 32:48, :].reshape(D, D)
        g = g_ref[:, columns]
        inter = jnp.concatenate([g * before, g * after], axis=1)
        dq = part_ref[0, h].astype(F32) + nt(inter, jnp.concatenate([enter, cached], axis=1))
        out_ref[0, h] = (dq * scale).astype(BF16)
        dk = part_ref[1, h].astype(F32) + nt(v_ref[:, columns] * final, leave)
        out_ref[1, h] = (dk * scale).astype(BF16)
        dv = part_ref[2, h].astype(F32) + nn(k_ref[:, columns] * final, leave)
        out_ref[2, h] = (dv * scale).astype(BF16)
        for n, far in enumerate((dq_any, dk_any, dv_any)):
            copy = pltpu.make_async_copy(out_ref.at[n, h], far.at[:, columns], out_sem.at[n, h])
            copy.start()
            copies.append(copy)
    for copy in copies:
        copy.wait()


def state_grads(session_start, key_rows, value_rows, out_grad, parts, states):
    _, heads, length, _ = parts.shape
    total = heads * D // PIECE
    hbm, vmem = whole(pltpu.HBM), whole(pltpu.VMEM)
    near = pltpu.VMEM((3, heads, length, D), BF16)
    wide = jax.ShapeDtypeStruct((length, heads * D), BF16)
    *grads, grad_cache = pl.pallas_call(
        state_kernel,
        in_specs=[hbm, vmem, vmem, vmem, hbm, hbm],
        out_specs=[hbm] * 4,
        out_shape=[wide, wide, wide, jax.ShapeDtypeStruct((total, PIECE, D), BF16)],
        scratch_shapes=[
            pltpu.SMEM(session_start.shape, jnp.int32),
            near,
            pltpu.VMEM(states.shape, BF16),
            near,
            pltpu.SemaphoreType.DMA(()),
            pltpu.SemaphoreType.DMA((heads,)),
            pltpu.SemaphoreType.DMA((heads,)),
            pltpu.SemaphoreType.DMA((heads,)),
            pltpu.SemaphoreType.DMA((3, heads)),
        ],
        compiler_params=pltpu.CompilerParams(vmem_limit_bytes=STATE_BYTES),
        cost_estimate=pl.CostEstimate(
            flops=8 * heads * length * D * D, bytes_accessed=20 * heads * length * D, transcendentals=0
        ),
        name="state_grads",
    )(session_start, key_rows, value_rows, out_grad, parts, states)
    return *grads, grad_cache.reshape(1, heads, D, D)


def shards(
    queries,
    key_rows,
    value_rows,
    out_grad,
    cache_states,
    session_start,
    cache_owner,
    probe_gate,
    steer_vector,
):
    heads = steer_vector.shape[0]
    sent, gate = block_sums(
        queries, key_rows, value_rows, out_grad, cache_states, session_start, probe_gate, steer_vector
    )
    pieces = lax.all_to_all(sent, "seq", 0, 0, tiled=True)
    parts = local_grads(session_start, queries, key_rows, value_rows, out_grad)
    pieces, parts = lax.optimization_barrier((pieces, parts))
    scanned, grad_steer = scan_blocks(cache_owner, pieces, heads)
    states = lax.all_to_all(scanned, "seq", 0, 0, tiled=True)
    grad_queries, grad_keys, grad_values, grad_cache = state_grads(
        session_start, key_rows, value_rows, out_grad, parts, states
    )
    count = lax.axis_size("head")
    step = 1
    while step < count:
        gate = gate + lax.ppermute(gate, "head", [(i, i ^ step) for i in range(count)])
        step *= 2
    return (grad_queries, grad_keys, grad_values, grad_cache, grad_steer, gate.reshape(-1))


def solution(mesh):
    in_specs = (
        P("seq", "head"),
        P("seq", "head"),
        P("seq", "head"),
        P("seq", "head"),
        P("seq", "head", None, None),
        P("seq"),
        P(),
        P("seq"),
        P("head", None),
    )
    out_specs = (
        P("seq", "head"),
        P("seq", "head"),
        P("seq", "head"),
        P("seq", "head", None, None),
        P("head", None),
        P("seq"),
    )
    return jax.shard_map(shards, mesh=mesh, in_specs=in_specs, out_specs=out_specs, check_vma=False)
```

```python
import functools
import math

import jax
import jax.numpy as jnp
from jax import lax
from jax.experimental import pallas as pl
from jax.experimental.pallas import tpu as pltpu
from jax.sharding import PartitionSpec as P

D = 128
PIECE = 16
STRIP = 256
VMEM_BYTES = 60 << 20
STATE_BYTES = 48 << 20
AHEAD = 2
F32 = jnp.float32
BF16 = jnp.bfloat16


def nt(a, b):
    return lax.dot_general(a, b, (((1,), (1,)), ((), ())), preferred_element_type=F32)


def nn(a, b):
    return lax.dot_general(a, b, (((1,), (0,)), ((), ())), preferred_element_type=F32)


def tn(a, b):
    return lax.dot_general(a, b, (((0,), (0,)), ((), ())), preferred_element_type=F32)


def group_place(b, count):
    return lax.rem(7 * count // 4 - 1 - b, count) if isinstance(b, jax.Array) else (7 * count // 4 - 1 - b) % count


def row_masks(start, length):
    rows = lax.broadcasted_iota(jnp.int32, (length, D), 0)
    after = (rows >= start).astype(F32)
    before = 1.0 - after
    whole = jnp.where(start >= length, 1.0, 0.0).astype(F32)
    final = jnp.maximum(after, whole)
    return before.astype(BF16), after.astype(BF16), final.astype(BF16)


def whole(space):
    return pl.BlockSpec(memory_space=space)


def sums_kernel(
    start_any, q_any, k_any, v_any, g_any, c_any, probe_any, steer_any, u_any, gate_ref,
    start_ref, q_ref, k_ref, v_ref, g_ref, probe_ref, steer_ref, u_ref, in_sem, few_sem, out_sem,
):
    heads, length, _ = q_ref.shape
    pieces = D // PIECE

    def fetches(h):
        pairs = ((k_any, k_ref), (v_any, v_ref), (q_any, q_ref), (g_any, g_ref))
        return [
            pltpu.make_async_copy(far.at[:, h * D : (h + 1) * D], near.at[h], in_sem.at[n, h])
            for n, (far, near) in enumerate(pairs)
        ]

    few = [
        pltpu.make_async_copy(start_any, start_ref, few_sem.at[0]),
        pltpu.make_async_copy(probe_any, probe_ref, few_sem.at[1]),
        pltpu.make_async_copy(steer_any, steer_ref, few_sem.at[2]),
    ]
    cached = pltpu.make_async_copy(c_any, u_ref.at[:, 16:32, :], few_sem.at[3])
    for copy in few:
        copy.start()
    for h in range(AHEAD):
        for copy in fetches(h):
            copy.start()
    cached.start()
    for copy in few:
        copy.wait()
    start = start_ref[0]
    before, after, final = row_masks(start, length)
    probe = probe_ref[...]
    high = probe.astype(BF16)
    low = (probe - high.astype(F32)).astype(BF16)
    steer = steer_ref[...].astype(F32)
    rows = lax.broadcasted_iota(jnp.int32, (8, D), 0)
    flag = jnp.where(start < length, 1.0, 0.0).astype(F32)
    tile = jnp.full((8, D), flag)
    gate = jnp.zeros((heads, length), F32)
    sent = []
    for h in range(heads):
        for copy in fetches(h):
            copy.wait()
        if h + AHEAD < heads:
            for copy in fetches(h + AHEAD):
                copy.start()
        g = g_ref[h]
        kv = tn(k_ref[h], v_ref[h] * final)
        both = tn(q_ref[h], jnp.concatenate([g * before, g * after], axis=1))
        here = slice(h * pieces, (h + 1) * pieces)
        u_ref[here, 0:16, :] = both[:, D:].astype(BF16).reshape(pieces, PIECE, D)
        u_ref[here, 32:48, :] = kv.astype(BF16).reshape(pieces, PIECE, D)
        u_ref[here, 48:64, :] = both[:, :D].astype(BF16).reshape(pieces, PIECE, D)
        if h == 0:
            cached.wait()
        copy = pltpu.make_async_copy(u_ref.at[here, 0:64, :], u_any.at[here, 0:64, :], out_sem.at[h])
        copy.start()
        sent.append(copy)
        steer_sum = nn(high, g) + nn(low, g)
        tile = jnp.where(rows == h, jnp.broadcast_to(steer_sum, (8, D)), tile)
        vector = jnp.where(rows[:heads] == h, steer, 0.0).astype(BF16)
        gate = gate + nt(vector, g)
    u_ref[:, 64:72, :] = jnp.broadcast_to(tile.astype(BF16)[None], (u_ref.shape[0], 8, D))
    copy = pltpu.make_async_copy(u_ref.at[:, 64:72, :], u_any.at[:, 64:72, :], out_sem.at[heads])
    copy.start()
    sent.append(copy)
    gate_ref[...] = jnp.sum(gate, axis=0, keepdims=True)
    for copy in sent:
        copy.wait()


def block_sums(queries, key_rows, value_rows, out_grad, cache_states, session_start, probe_gate, steer_vector):
    length, width = queries.shape
    heads = width // D
    total = heads * D // PIECE
    near = pltpu.VMEM((heads, length, D), BF16)
    hbm, vmem = whole(pltpu.HBM), whole(pltpu.VMEM)
    return pl.pallas_call(
        sums_kernel,
        in_specs=[hbm] * 8,
        out_specs=[hbm, vmem],
        out_shape=[
            jax.ShapeDtypeStruct((total, 72, D), BF16),
            jax.ShapeDtypeStruct((1, length), F32),
        ],
        scratch_shapes=[
            pltpu.SMEM(session_start.shape, jnp.int32),
            near,
            near,
            near,
            near,
            pltpu.VMEM((1, length), F32),
            pltpu.VMEM(steer_vector.shape, BF16),
            pltpu.VMEM((total, 72, D), BF16),
            pltpu.SemaphoreType.DMA((4, heads)),
            pltpu.SemaphoreType.DMA((4,)),
            pltpu.SemaphoreType.DMA((heads + 1,)),
        ],
        compiler_params=pltpu.CompilerParams(vmem_limit_bytes=VMEM_BYTES),
        cost_estimate=pl.CostEstimate(
            flops=8 * heads * length * D * D, bytes_accessed=8 * length * width, transcendentals=0
        ),
        name="block_sums",
    )(
        session_start,
        queries,
        key_rows,
        value_rows,
        out_grad,
        cache_states.reshape(total, PIECE, D),
        probe_gate.reshape(1, length),
        steer_vector,
    )


def scan_kernel(owner_any, v_any, w_any, steer_ref, owner_ref, v_ref, w_ref, in_sem, out_sem):
    blocks = v_ref.shape[0]
    fetched = [pltpu.make_async_copy(owner_any, owner_ref, in_sem.at[0])]
    for n, rows in enumerate((slice(16, 48), slice(64, 72), slice(0, 16), slice(48, 64))):
        fetched.append(pltpu.make_async_copy(v_any.at[:, rows, :], v_ref.at[:, rows, :], in_sem.at[n + 1]))
    for copy in fetched:
        copy.start()

    def extra(b):
        return v_ref[group_place(b, blocks), 64:72, :].astype(F32)

    def flag_of(b):
        row = extra(b)[4:5]
        return jnp.broadcast_to(row, (PIECE, D)) > 0.5

    state = jnp.zeros((PIECE, D), F32)
    steer = jnp.zeros((8, D), F32)
    for copy in fetched[:3]:
        copy.wait()
    for b in range(blocks):
        here = group_place(b, blocks)
        cached = v_ref[group_place(owner_ref[b], blocks), 16:32, :]
        w_ref[here, 0:16, :] = state.astype(BF16)
        w_ref[here, 16:32, :] = cached
        added = v_ref[here, 32:48, :].astype(F32)
        state = added + jnp.where(flag_of(b), cached.astype(F32), state)
        steer = steer + extra(b)
    first = pltpu.make_async_copy(w_ref.at[:, 0:32, :], w_any.at[:, 0:32, :], out_sem.at[0])
    first.start()
    for copy in fetched[3:]:
        copy.wait()
    state = jnp.zeros((PIECE, D), F32)
    for b in reversed(range(blocks)):
        here = group_place(b, blocks)
        flag = flag_of(b)
        w_ref[here, 32:48, :] = state.astype(BF16)
        begun = (v_ref[here, 0:16, :].astype(F32) + state) * (1.0 / D)
        slot = group_place(owner_ref[b], blocks)
        w_ref[slot, 48:64, :] = jnp.where(flag, begun, 0.0).astype(BF16)
        state = v_ref[here, 48:64, :].astype(F32) + jnp.where(flag, 0.0, state)
    second = pltpu.make_async_copy(w_ref.at[:, 32:64, :], w_any.at[:, 32:64, :], out_sem.at[1])
    second.start()
    tokens = blocks * 1024
    steer_ref[...] = steer[0 : steer_ref.shape[0]] * (1.0 / math.sqrt(tokens))
    first.wait()
    second.wait()


def scan_blocks(owner, pieces, heads):
    blocks = pieces.shape[0]
    hbm, vmem = whole(pltpu.HBM), whole(pltpu.VMEM)
    return pl.pallas_call(
        scan_kernel,
        in_specs=[hbm, hbm],
        out_specs=[hbm, vmem],
        out_shape=[
            jax.ShapeDtypeStruct((blocks, 64, D), BF16),
            jax.ShapeDtypeStruct((heads, D), F32),
        ],
        scratch_shapes=[
            pltpu.SMEM(owner.shape, jnp.int32),
            pltpu.VMEM(pieces.shape, BF16),
            pltpu.VMEM((blocks, 64, D), BF16),
            pltpu.SemaphoreType.DMA((5,)),
            pltpu.SemaphoreType.DMA((2,)),
        ],
        compiler_params=pltpu.CompilerParams(vmem_limit_bytes=VMEM_BYTES),
        name="scan_blocks",
    )(owner, pieces)


def local_kernel(
    start_any, q_any, k_any, v_any, g_any, part_any,
    start_ref, q_ref, k_ref, v_ref, g_ref, part_ref, start_sem, in_sem, out_sem,
):
    heads, length, _ = q_ref.shape
    started = pltpu.make_async_copy(start_any, start_ref, start_sem)
    started.start()

    def fetches(h):
        pairs = ((g_any, g_ref), (v_any, v_ref), (k_any, k_ref), (q_any, q_ref))
        columns = pl.ds(pl.multiple_of(h * D, D), D)
        return [
            pltpu.make_async_copy(far.at[:, columns], near.at[h], in_sem.at[n, h])
            for n, (far, near) in enumerate(pairs)
        ]

    def result(h):
        return pltpu.make_async_copy(part_ref.at[:, h], part_any.at[:, h], out_sem.at[h])

    for h in range(AHEAD):
        for copy in fetches(h):
            copy.start()

    started.wait()
    start = start_ref[0]

    @pl.loop(0, heads)
    def _(h):
        for copy in fetches(h):
            copy.wait()

        @pl.when(h + AHEAD < heads)
        def _():
            for copy in fetches(h + AHEAD):
                copy.start()

        for i in range(length // STRIP):
            lo, hi = i * STRIP, (i + 1) * STRIP
            s = lo + lax.broadcasted_iota(jnp.int32, (STRIP, hi), 0)
            t = lax.broadcasted_iota(jnp.int32, (STRIP, hi), 1)
            keep = (t <= s) & (t >= jnp.where(s >= start, start, 0))
            y = jnp.where(keep, nt(g_ref[h, lo:hi, :], v_ref[h, 0:hi, :]), 0.0).astype(BF16)
            part_ref[0, h, lo:hi, :] = nn(y, k_ref[h, 0:hi, :]).astype(BF16)
        for j in range(length // STRIP):
            lo, hi = j * STRIP, (j + 1) * STRIP
            rest = length - lo
            t = lo + lax.broadcasted_iota(jnp.int32, (STRIP, rest), 0)
            s = lo + lax.broadcasted_iota(jnp.int32, (STRIP, rest), 1)
            keep = (t <= s) & (s < jnp.where(t < start, start, length))
            yt = jnp.where(keep, nt(v_ref[h, lo:hi, :], g_ref[h, lo:length, :]), 0.0).astype(BF16)
            part_ref[1, h, lo:hi, :] = nn(yt, q_ref[h, lo:length, :]).astype(BF16)
            xt = jnp.where(keep, nt(k_ref[h, lo:hi, :], q_ref[h, lo:length, :]), 0.0).astype(BF16)
            part_ref[2, h, lo:hi, :] = nn(xt, g_ref[h, lo:length, :]).astype(BF16)
        result(h).start()

    for h in range(heads):
        result(h).wait()


def local_grads(session_start, queries, key_rows, value_rows, out_grad):
    length, width = queries.shape
    heads = width // D
    hbm = whole(pltpu.HBM)
    near = pltpu.VMEM((heads, length, D), BF16)
    return pl.pallas_call(
        local_kernel,
        in_specs=[hbm] * 5,
        out_specs=hbm,
        out_shape=jax.ShapeDtypeStruct((3, heads, length, D), BF16),
        scratch_shapes=[pltpu.SMEM(session_start.shape, jnp.int32)]
        + [near] * 4
        + [
            pltpu.VMEM((3, heads, length, D), BF16),
            pltpu.SemaphoreType.DMA(()),
            pltpu.SemaphoreType.DMA((4, heads)),
            pltpu.SemaphoreType.DMA((heads,)),
        ],
        compiler_params=pltpu.CompilerParams(vmem_limit_bytes=VMEM_BYTES),
        cost_estimate=pl.CostEstimate(
            flops=16 * heads * length * length * D, bytes_accessed=20 * heads * length * D, transcendentals=0
        ),
        name="local_grads",
    )(session_start, queries, key_rows, value_rows, out_grad)


def state_kernel(
    start_any, k_ref, v_ref, g_ref, part_any, w_any,
    dq_any, dk_any, dv_any, dc_any,
    start_ref, part_ref, w_ref, out_ref, start_sem, in_sem, w_sem, c_sem, out_sem,
):
    _, heads, length, _ = part_ref.shape
    pieces = D // PIECE

    def fetch(h):
        return pltpu.make_async_copy(part_any.at[:, h], part_ref.at[:, h], in_sem.at[h])

    def states(h):
        here = slice(h * pieces, (h + 1) * pieces)
        return pltpu.make_async_copy(w_any.at[here], w_ref.at[here], w_sem.at[h])

    def cache(h):
        here = slice(h * pieces, (h + 1) * pieces)
        return pltpu.make_async_copy(w_ref.at[here, 48:64, :], dc_any.at[here], c_sem.at[h])

    started = pltpu.make_async_copy(start_any, start_ref, start_sem)
    started.start()
    for h in range(AHEAD):
        states(h).start()
        fetch(h).start()
    copies = []
    started.wait()
    start = start_ref[0]
    before, after, final = row_masks(start, length)
    scale = 1.0 / D
    for h in range(heads):
        fetch(h).wait()
        states(h).wait()
        if h + AHEAD < heads:
            states(h + AHEAD).start()
            fetch(h + AHEAD).start()
        cache(h).start()
        copies.append(cache(h))
        columns = slice(h * D, (h + 1) * D)
        here = slice(h * pieces, (h + 1) * pieces)
        enter = w_ref[here, 0:16, :].reshape(D, D)
        cached = w_ref[here, 16:32, :].reshape(D, D)
        leave = w_ref[here, 32:48, :].reshape(D, D)
        g = g_ref[:, columns]
        inter = jnp.concatenate([g * before, g * after], axis=1)
        dq = part_ref[0, h].astype(F32) + nt(inter, jnp.concatenate([enter, cached], axis=1))
        out_ref[0, h] = (dq * scale).astype(BF16)
        dk = part_ref[1, h].astype(F32) + nt(v_ref[:, columns] * final, leave)
        out_ref[1, h] = (dk * scale).astype(BF16)
        dv = part_ref[2, h].astype(F32) + nn(k_ref[:, columns] * final, leave)
        out_ref[2, h] = (dv * scale).astype(BF16)
        for n, far in enumerate((dq_any, dk_any, dv_any)):
            copy = pltpu.make_async_copy(out_ref.at[n, h], far.at[:, columns], out_sem.at[n, h])
            copy.start()
            copies.append(copy)
    for copy in copies:
        copy.wait()


def state_grads(session_start, key_rows, value_rows, out_grad, parts, states):
    _, heads, length, _ = parts.shape
    total = heads * D // PIECE
    hbm, vmem = whole(pltpu.HBM), whole(pltpu.VMEM)
    near = pltpu.VMEM((3, heads, length, D), BF16)
    wide = jax.ShapeDtypeStruct((length, heads * D), BF16)
    *grads, grad_cache = pl.pallas_call(
        state_kernel,
        in_specs=[hbm, vmem, vmem, vmem, hbm, hbm],
        out_specs=[hbm] * 4,
        out_shape=[wide, wide, wide, jax.ShapeDtypeStruct((total, PIECE, D), BF16)],
        scratch_shapes=[
            pltpu.SMEM(session_start.shape, jnp.int32),
            near,
            pltpu.VMEM(states.shape, BF16),
            near,
            pltpu.SemaphoreType.DMA(()),
            pltpu.SemaphoreType.DMA((heads,)),
            pltpu.SemaphoreType.DMA((heads,)),
            pltpu.SemaphoreType.DMA((heads,)),
            pltpu.SemaphoreType.DMA((3, heads)),
        ],
        compiler_params=pltpu.CompilerParams(vmem_limit_bytes=STATE_BYTES),
        cost_estimate=pl.CostEstimate(
            flops=8 * heads * length * D * D, bytes_accessed=20 * heads * length * D, transcendentals=0
        ),
        name="state_grads",
    )(session_start, key_rows, value_rows, out_grad, parts, states)
    return *grads, grad_cache.reshape(1, heads, D, D)


def shards(
    queries,
    key_rows,
    value_rows,
    out_grad,
    cache_states,
    session_start,
    cache_owner,
    probe_gate,
    steer_vector,
):
    heads = steer_vector.shape[0]
    sent, gate = block_sums(
        queries, key_rows, value_rows, out_grad, cache_states, session_start, probe_gate, steer_vector
    )
    blocks = lax.axis_size("seq")
    group = [sorted(range(blocks), key=lambda b: group_place(b, blocks))]
    pieces = lax.all_to_all(sent, "seq", 0, 0, tiled=True, axis_index_groups=group)
    parts = local_grads(session_start, queries, key_rows, value_rows, out_grad)
    pieces, parts = lax.optimization_barrier((pieces, parts))
    scanned, grad_steer = scan_blocks(cache_owner, pieces, heads)
    states = lax.all_to_all(scanned, "seq", 0, 0, tiled=True, axis_index_groups=group)
    grad_queries, grad_keys, grad_values, grad_cache = state_grads(
        session_start, key_rows, value_rows, out_grad, parts, states
    )
    count = lax.axis_size("head")
    step = 1
    while step < count:
        gate = gate + lax.ppermute(gate, "head", [(i, i ^ step) for i in range(count)])
        step *= 2
    return (grad_queries, grad_keys, grad_values, grad_cache, grad_steer, gate.reshape(-1))


def solution(mesh):
    in_specs = (
        P("seq", "head"),
        P("seq", "head"),
        P("seq", "head"),
        P("seq", "head"),
        P("seq", "head", None, None),
        P("seq"),
        P(),
        P("seq"),
        P("head", None),
    )
    out_specs = (
        P("seq", "head"),
        P("seq", "head"),
        P("seq", "head"),
        P("seq", "head", None, None),
        P("head", None),
        P("seq"),
    )
    return jax.shard_map(shards, mesh=mesh, in_specs=in_specs, out_specs=out_specs, check_vma=False)
```

```python
import functools
import math

import jax
import jax.numpy as jnp
from jax import lax
from jax.experimental import pallas as pl
from jax.experimental.pallas import tpu as pltpu
from jax.sharding import PartitionSpec as P

D = 128
PIECE = 16
STRIP = 256
VMEM_BYTES = 60 << 20
STATE_BYTES = 48 << 20
AHEAD = 2
F32 = jnp.float32
BF16 = jnp.bfloat16


def nt(a, b):
    return lax.dot_general(a, b, (((1,), (1,)), ((), ())), preferred_element_type=F32)


def nn(a, b):
    return lax.dot_general(a, b, (((1,), (0,)), ((), ())), preferred_element_type=F32)


def tn(a, b):
    return lax.dot_general(a, b, (((0,), (0,)), ((), ())), preferred_element_type=F32)


def group_place(b, count):
    return lax.rem(7 * count // 4 - 1 - b, count) if isinstance(b, jax.Array) else (7 * count // 4 - 1 - b) % count


def row_masks(start, length):
    rows = lax.broadcasted_iota(jnp.int32, (length, D), 0)
    after = (rows >= start).astype(F32)
    before = 1.0 - after
    whole = jnp.where(start >= length, 1.0, 0.0).astype(F32)
    final = jnp.maximum(after, whole)
    return before.astype(BF16), after.astype(BF16), final.astype(BF16)


def whole(space):
    return pl.BlockSpec(memory_space=space)


def sums_kernel(
    start_any, q_any, k_any, v_any, g_any, c_any, probe_any, steer_any, u_any, gate_ref,
    start_ref, q_ref, k_ref, v_ref, g_ref, probe_ref, steer_ref, u_ref, in_sem, few_sem, out_sem,
):
    heads, length, _ = q_ref.shape
    pieces = D // PIECE

    def fetches(h):
        pairs = ((k_any, k_ref), (v_any, v_ref), (q_any, q_ref), (g_any, g_ref))
        return [
            pltpu.make_async_copy(far.at[:, h * D : (h + 1) * D], near.at[h], in_sem.at[n, h])
            for n, (far, near) in enumerate(pairs)
        ]

    few = [
        pltpu.make_async_copy(start_any, start_ref, few_sem.at[0]),
        pltpu.make_async_copy(probe_any, probe_ref, few_sem.at[1]),
        pltpu.make_async_copy(steer_any, steer_ref, few_sem.at[2]),
    ]
    cached = pltpu.make_async_copy(c_any, u_ref.at[:, 32:48, :], few_sem.at[3])
    for copy in few:
        copy.start()
    for h in range(AHEAD):
        for copy in fetches(h):
            copy.start()
    cached.start()
    for copy in few:
        copy.wait()
    start = start_ref[0]
    before, after, final = row_masks(start, length)
    probe = probe_ref[...]
    high = probe.astype(BF16)
    low = (probe - high.astype(F32)).astype(BF16)
    steer = steer_ref[...].astype(F32)
    rows = lax.broadcasted_iota(jnp.int32, (8, D), 0)
    flag = jnp.where(start < length, 1.0, 0.0).astype(F32)
    tile = jnp.full((8, D), flag)
    gate = jnp.zeros((heads, length), F32)
    sent = []
    for h in range(heads):
        for copy in fetches(h):
            copy.wait()
        if h + AHEAD < heads:
            for copy in fetches(h + AHEAD):
                copy.start()
        g = g_ref[h]
        kv = tn(k_ref[h], v_ref[h] * final)
        both = tn(q_ref[h], jnp.concatenate([g * before, g * after], axis=1))
        here = slice(h * pieces, (h + 1) * pieces)
        u_ref[here, 16:32, :] = both[:, D:].astype(BF16).reshape(pieces, PIECE, D)
        u_ref[here, 48:64, :] = kv.astype(BF16).reshape(pieces, PIECE, D)
        u_ref[here, 0:16, :] = both[:, :D].astype(BF16).reshape(pieces, PIECE, D)
        if h == 0:
            cached.wait()
        copy = pltpu.make_async_copy(u_ref.at[here, 0:64, :], u_any.at[here, 0:64, :], out_sem.at[h])
        copy.start()
        sent.append(copy)
        steer_sum = nn(high, g) + nn(low, g)
        tile = jnp.where(rows == h, jnp.broadcast_to(steer_sum, (8, D)), tile)
        vector = jnp.where(rows[:heads] == h, steer, 0.0).astype(BF16)
        gate = gate + nt(vector, g)
    u_ref[:, 64:72, :] = jnp.broadcast_to(tile.astype(BF16)[None], (u_ref.shape[0], 8, D))
    copy = pltpu.make_async_copy(u_ref.at[:, 64:72, :], u_any.at[:, 64:72, :], out_sem.at[heads])
    copy.start()
    sent.append(copy)
    gate_ref[...] = jnp.sum(gate, axis=0, keepdims=True)
    for copy in sent:
        copy.wait()


def block_sums(queries, key_rows, value_rows, out_grad, cache_states, session_start, probe_gate, steer_vector):
    length, width = queries.shape
    heads = width // D
    total = heads * D // PIECE
    near = pltpu.VMEM((heads, length, D), BF16)
    hbm, vmem = whole(pltpu.HBM), whole(pltpu.VMEM)
    return pl.pallas_call(
        sums_kernel,
        in_specs=[hbm] * 8,
        out_specs=[hbm, vmem],
        out_shape=[
            jax.ShapeDtypeStruct((total, 72, D), BF16),
            jax.ShapeDtypeStruct((1, length), F32),
        ],
        scratch_shapes=[
            pltpu.SMEM(session_start.shape, jnp.int32),
            near,
            near,
            near,
            near,
            pltpu.VMEM((1, length), F32),
            pltpu.VMEM(steer_vector.shape, BF16),
            pltpu.VMEM((total, 72, D), BF16),
            pltpu.SemaphoreType.DMA((4, heads)),
            pltpu.SemaphoreType.DMA((4,)),
            pltpu.SemaphoreType.DMA((heads + 1,)),
        ],
        compiler_params=pltpu.CompilerParams(vmem_limit_bytes=VMEM_BYTES),
        cost_estimate=pl.CostEstimate(
            flops=8 * heads * length * D * D, bytes_accessed=8 * length * width, transcendentals=0
        ),
        name="block_sums",
    )(
        session_start,
        queries,
        key_rows,
        value_rows,
        out_grad,
        cache_states.reshape(total, PIECE, D),
        probe_gate.reshape(1, length),
        steer_vector,
    )


def scan_kernel(owner_any, v_any, w_any, steer_ref, owner_ref, v_ref, w_ref, in_sem, out_sem):
    blocks = v_ref.shape[0]
    fetched = [pltpu.make_async_copy(owner_any, owner_ref, in_sem.at[0])]
    for n, rows in enumerate((slice(16, 72), slice(0, 16))):
        fetched.append(pltpu.make_async_copy(v_any.at[:, rows, :], v_ref.at[:, rows, :], in_sem.at[n + 1]))
    for copy in fetched:
        copy.start()

    def extra(b):
        return v_ref[group_place(b, blocks), 64:72, :].astype(F32)

    def flag_of(b):
        row = extra(b)[4:5]
        return jnp.broadcast_to(row, (PIECE, D)) > 0.5

    state = jnp.zeros((PIECE, D), F32)
    steer = jnp.zeros((8, D), F32)
    for copy in fetched[:2]:
        copy.wait()
    for b in range(blocks):
        here = group_place(b, blocks)
        cached = v_ref[group_place(owner_ref[b], blocks), 32:48, :]
        w_ref[here, 0:16, :] = state.astype(BF16)
        w_ref[here, 16:32, :] = cached
        added = v_ref[here, 48:64, :].astype(F32)
        state = added + jnp.where(flag_of(b), cached.astype(F32), state)
        steer = steer + extra(b)
    first = pltpu.make_async_copy(w_ref.at[:, 0:32, :], w_any.at[:, 0:32, :], out_sem.at[0])
    first.start()
    for copy in fetched[2:]:
        copy.wait()
    state = jnp.zeros((PIECE, D), F32)
    for b in reversed(range(blocks)):
        here = group_place(b, blocks)
        flag = flag_of(b)
        w_ref[here, 32:48, :] = state.astype(BF16)
        begun = (v_ref[here, 16:32, :].astype(F32) + state) * (1.0 / D)
        slot = group_place(owner_ref[b], blocks)
        w_ref[slot, 48:64, :] = jnp.where(flag, begun, 0.0).astype(BF16)
        state = v_ref[here, 0:16, :].astype(F32) + jnp.where(flag, 0.0, state)
    second = pltpu.make_async_copy(w_ref.at[:, 32:64, :], w_any.at[:, 32:64, :], out_sem.at[1])
    second.start()
    tokens = blocks * 1024
    steer_ref[...] = steer[0 : steer_ref.shape[0]] * (1.0 / math.sqrt(tokens))
    first.wait()
    second.wait()


def scan_blocks(owner, pieces, heads):
    blocks = pieces.shape[0]
    hbm, vmem = whole(pltpu.HBM), whole(pltpu.VMEM)
    return pl.pallas_call(
        scan_kernel,
        in_specs=[hbm, hbm],
        out_specs=[hbm, vmem],
        out_shape=[
            jax.ShapeDtypeStruct((blocks, 64, D), BF16),
            jax.ShapeDtypeStruct((heads, D), F32),
        ],
        scratch_shapes=[
            pltpu.SMEM(owner.shape, jnp.int32),
            pltpu.VMEM(pieces.shape, BF16),
            pltpu.VMEM((blocks, 64, D), BF16),
            pltpu.SemaphoreType.DMA((3,)),
            pltpu.SemaphoreType.DMA((2,)),
        ],
        compiler_params=pltpu.CompilerParams(vmem_limit_bytes=VMEM_BYTES),
        name="scan_blocks",
    )(owner, pieces)


def local_kernel(
    start_any, q_any, k_any, v_any, g_any, part_any,
    start_ref, q_ref, k_ref, v_ref, g_ref, sum_ref, part_ref, start_sem, in_sem, out_sem,
):
    heads, length, _ = q_ref.shape
    started = pltpu.make_async_copy(start_any, start_ref, start_sem)
    started.start()

    def fetches(h):
        pairs = ((g_any, g_ref), (v_any, v_ref), (k_any, k_ref), (q_any, q_ref))
        columns = pl.ds(pl.multiple_of(h * D, D), D)
        return [
            pltpu.make_async_copy(far.at[:, columns], near.at[h], in_sem.at[n, h])
            for n, (far, near) in enumerate(pairs)
        ]

    def result(h):
        return pltpu.make_async_copy(part_ref.at[:, h], part_any.at[:, h], out_sem.at[h])

    for h in range(AHEAD):
        for copy in fetches(h):
            copy.start()

    started.wait()
    start = start_ref[0]

    @pl.loop(0, heads)
    def _(h):
        for copy in fetches(h):
            copy.wait()

        @pl.when(h + AHEAD < heads)
        def _():
            for copy in fetches(h + AHEAD):
                copy.start()

        for i in range(length // STRIP):
            lo, hi = i * STRIP, (i + 1) * STRIP
            s = lo + lax.broadcasted_iota(jnp.int32, (STRIP, hi), 0)
            t = lax.broadcasted_iota(jnp.int32, (STRIP, hi), 1)
            keep = (t <= s) & (t >= jnp.where(s >= start, start, 0))
            g = g_ref[h, lo:hi, :]
            q = q_ref[h, lo:hi, :]
            y = jnp.where(keep, nt(g, v_ref[h, 0:hi, :]), 0.0).astype(BF16)
            part_ref[0, h, lo:hi, :] = nn(y, k_ref[h, 0:hi, :]).astype(BF16)
            x = jnp.where(keep, nt(q, k_ref[h, 0:hi, :]), 0.0).astype(BF16)
            dk = tn(y, q)
            dv = tn(x, g)
            sum_ref[0, lo:hi, :] = dk[lo:]
            sum_ref[1, lo:hi, :] = dv[lo:]
            if i > 0:
                sum_ref[0, 0:lo, :] += dk[:lo]
                sum_ref[1, 0:lo, :] += dv[:lo]
        part_ref[1, h] = sum_ref[0].astype(BF16)
        part_ref[2, h] = sum_ref[1].astype(BF16)
        result(h).start()

    for h in range(heads):
        result(h).wait()


def local_grads(session_start, queries, key_rows, value_rows, out_grad):
    length, width = queries.shape
    heads = width // D
    hbm = whole(pltpu.HBM)
    near = pltpu.VMEM((heads, length, D), BF16)
    return pl.pallas_call(
        local_kernel,
        in_specs=[hbm] * 5,
        out_specs=hbm,
        out_shape=jax.ShapeDtypeStruct((3, heads, length, D), BF16),
        scratch_shapes=[pltpu.SMEM(session_start.shape, jnp.int32)]
        + [near] * 4
        + [
            pltpu.VMEM((2, length, D), F32),
            pltpu.VMEM((3, heads, length, D), BF16),
            pltpu.SemaphoreType.DMA(()),
            pltpu.SemaphoreType.DMA((4, heads)),
            pltpu.SemaphoreType.DMA((heads,)),
        ],
        compiler_params=pltpu.CompilerParams(vmem_limit_bytes=VMEM_BYTES),
        cost_estimate=pl.CostEstimate(
            flops=16 * heads * length * length * D, bytes_accessed=20 * heads * length * D, transcendentals=0
        ),
        name="local_grads",
    )(session_start, queries, key_rows, value_rows, out_grad)


def state_kernel(
    start_any, k_ref, v_ref, g_ref, part_any, w_any,
    dq_any, dk_any, dv_any, dc_any,
    start_ref, part_ref, w_ref, out_ref, start_sem, in_sem, w_sem, c_sem, out_sem,
):
    _, heads, length, _ = part_ref.shape
    pieces = D // PIECE

    def fetch(h):
        return pltpu.make_async_copy(part_any.at[:, h], part_ref.at[:, h], in_sem.at[h])

    def states(h):
        here = slice(h * pieces, (h + 1) * pieces)
        return pltpu.make_async_copy(w_any.at[here], w_ref.at[here], w_sem.at[h])

    def cache(h):
        here = slice(h * pieces, (h + 1) * pieces)
        return pltpu.make_async_copy(w_ref.at[here, 48:64, :], dc_any.at[here], c_sem.at[h])

    started = pltpu.make_async_copy(start_any, start_ref, start_sem)
    started.start()
    for h in range(heads):
        states(h).start()
        fetch(h).start()
    copies = []
    started.wait()
    start = start_ref[0]
    before, after, final = row_masks(start, length)
    scale = 1.0 / D
    for h in range(heads):
        fetch(h).wait()
        states(h).wait()
        cache(h).start()
        copies.append(cache(h))
        columns = slice(h * D, (h + 1) * D)
        here = slice(h * pieces, (h + 1) * pieces)
        enter = w_ref[here, 0:16, :].reshape(D, D)
        cached = w_ref[here, 16:32, :].reshape(D, D)
        leave = w_ref[here, 32:48, :].reshape(D, D)
        g = g_ref[:, columns]
        inter = jnp.concatenate([g * before, g * after], axis=1)
        dq = part_ref[0, h].astype(F32) + nt(inter, jnp.concatenate([enter, cached], axis=1))
        out_ref[0, h] = (dq * scale).astype(BF16)
        dk = part_ref[1, h].astype(F32) + nt(v_ref[:, columns] * final, leave)
        out_ref[1, h] = (dk * scale).astype(BF16)
        dv = part_ref[2, h].astype(F32) + nn(k_ref[:, columns] * final, leave)
        out_ref[2, h] = (dv * scale).astype(BF16)
        for n, far in enumerate((dq_any, dk_any, dv_any)):
            copy = pltpu.make_async_copy(out_ref.at[n, h], far.at[:, columns], out_sem.at[n, h])
            copy.start()
            copies.append(copy)
    for copy in copies:
        copy.wait()


def state_grads(session_start, key_rows, value_rows, out_grad, parts, states):
    _, heads, length, _ = parts.shape
    total = heads * D // PIECE
    hbm, vmem = whole(pltpu.HBM), whole(pltpu.VMEM)
    near = pltpu.VMEM((3, heads, length, D), BF16)
    wide = jax.ShapeDtypeStruct((length, heads * D), BF16)
    *grads, grad_cache = pl.pallas_call(
        state_kernel,
        in_specs=[hbm, vmem, vmem, vmem, hbm, hbm],
        out_specs=[hbm] * 4,
        out_shape=[wide, wide, wide, jax.ShapeDtypeStruct((total, PIECE, D), BF16)],
        scratch_shapes=[
            pltpu.SMEM(session_start.shape, jnp.int32),
            near,
            pltpu.VMEM(states.shape, BF16),
            near,
            pltpu.SemaphoreType.DMA(()),
            pltpu.SemaphoreType.DMA((heads,)),
            pltpu.SemaphoreType.DMA((heads,)),
            pltpu.SemaphoreType.DMA((heads,)),
            pltpu.SemaphoreType.DMA((3, heads)),
        ],
        compiler_params=pltpu.CompilerParams(vmem_limit_bytes=STATE_BYTES),
        cost_estimate=pl.CostEstimate(
            flops=8 * heads * length * D * D, bytes_accessed=20 * heads * length * D, transcendentals=0
        ),
        name="state_grads",
    )(session_start, key_rows, value_rows, out_grad, parts, states)
    return *grads, grad_cache.reshape(1, heads, D, D)


def shards(
    queries,
    key_rows,
    value_rows,
    out_grad,
    cache_states,
    session_start,
    cache_owner,
    probe_gate,
    steer_vector,
):
    heads = steer_vector.shape[0]
    sent, gate = block_sums(
        queries, key_rows, value_rows, out_grad, cache_states, session_start, probe_gate, steer_vector
    )
    blocks = lax.axis_size("seq")
    group = [sorted(range(blocks), key=lambda b: group_place(b, blocks))]
    pieces = lax.all_to_all(sent, "seq", 0, 0, tiled=True, axis_index_groups=group)
    parts = local_grads(session_start, queries, key_rows, value_rows, out_grad)
    pieces, parts = lax.optimization_barrier((pieces, parts))
    scanned, grad_steer = scan_blocks(cache_owner, pieces, heads)
    states = lax.all_to_all(scanned, "seq", 0, 0, tiled=True, axis_index_groups=group)
    grad_queries, grad_keys, grad_values, grad_cache = state_grads(
        session_start, key_rows, value_rows, out_grad, parts, states
    )
    count = lax.axis_size("head")
    step = 1
    while step < count:
        gate = gate + lax.ppermute(gate, "head", [(i, i ^ step) for i in range(count)])
        step *= 2
    return (grad_queries, grad_keys, grad_values, grad_cache, grad_steer, gate.reshape(-1))


def solution(mesh):
    in_specs = (
        P("seq", "head"),
        P("seq", "head"),
        P("seq", "head"),
        P("seq", "head"),
        P("seq", "head", None, None),
        P("seq"),
        P(),
        P("seq"),
        P("head", None),
    )
    out_specs = (
        P("seq", "head"),
        P("seq", "head"),
        P("seq", "head"),
        P("seq", "head", None, None),
        P("head", None),
        P("seq"),
    )
    return jax.shard_map(shards, mesh=mesh, in_specs=in_specs, out_specs=out_specs, check_vma=False)
```

```python
import functools
import math

import jax
import jax.numpy as jnp
from jax import lax
from jax.experimental import pallas as pl
from jax.experimental.pallas import tpu as pltpu
from jax.sharding import PartitionSpec as P

D = 128
PIECE = 16
STRIP = 256
VMEM_BYTES = 60 << 20
STATE_BYTES = 48 << 20
AHEAD = 2
NONE = 1e30
F32 = jnp.float32
BF16 = jnp.bfloat16


def nt(a, b):
    return lax.dot_general(a, b, (((1,), (1,)), ((), ())), preferred_element_type=F32)


def nn(a, b):
    return lax.dot_general(a, b, (((1,), (0,)), ((), ())), preferred_element_type=F32)


def tn(a, b):
    return lax.dot_general(a, b, (((0,), (0,)), ((), ())), preferred_element_type=F32)


def group_place(b, count):
    return lax.rem(7 * count // 4 - 1 - b, count) if isinstance(b, jax.Array) else (7 * count // 4 - 1 - b) % count


def row_masks(start, length):
    rows = lax.broadcasted_iota(jnp.int32, (length, D), 0)
    after = (rows >= start).astype(F32)
    before = 1.0 - after
    whole = jnp.where(start >= length, 1.0, 0.0).astype(F32)
    final = jnp.maximum(after, whole)
    return before.astype(BF16), after.astype(BF16), final.astype(BF16)


def whole(space):
    return pl.BlockSpec(memory_space=space)


def sums_kernel(
    start_any, q_any, k_any, v_any, g_any, c_any, probe_any, steer_any, u_any, gate_ref,
    start_ref, q_ref, k_ref, v_ref, g_ref, probe_ref, steer_ref, u_ref, in_sem, few_sem, out_sem,
):
    heads, length, _ = q_ref.shape
    pieces = D // PIECE

    def fetches(h):
        pairs = ((k_any, k_ref), (v_any, v_ref), (q_any, q_ref), (g_any, g_ref))
        return [
            pltpu.make_async_copy(far.at[:, h * D : (h + 1) * D], near.at[h], in_sem.at[n, h])
            for n, (far, near) in enumerate(pairs)
        ]

    few = [
        pltpu.make_async_copy(start_any, start_ref, few_sem.at[0]),
        pltpu.make_async_copy(probe_any, probe_ref, few_sem.at[1]),
        pltpu.make_async_copy(steer_any, steer_ref, few_sem.at[2]),
    ]
    cached = pltpu.make_async_copy(c_any, u_ref.at[:, 32:48, :], few_sem.at[3])
    for copy in few:
        copy.start()
    for h in range(AHEAD):
        for copy in fetches(h):
            copy.start()
    cached.start()
    for copy in few:
        copy.wait()
    start = start_ref[0]
    before, after, final = row_masks(start, length)
    probe = probe_ref[...]
    high = probe.astype(BF16)
    low = (probe - high.astype(F32)).astype(BF16)
    steer = steer_ref[...].astype(F32)
    rows = lax.broadcasted_iota(jnp.int32, (8, D), 0)
    tile = jnp.zeros((8, D), F32)
    gate = jnp.zeros((heads, length), F32)
    sent = []
    for h in range(heads):
        for copy in fetches(h):
            copy.wait()
        if h + AHEAD < heads:
            for copy in fetches(h + AHEAD):
                copy.start()
        g = g_ref[h]
        kv = tn(k_ref[h], v_ref[h] * final)
        both = tn(q_ref[h], jnp.concatenate([g * before, g * after], axis=1))
        here = slice(h * pieces, (h + 1) * pieces)
        begun = jnp.where(start < length, both[:, D:], NONE)
        u_ref[here, 16:32, :] = begun.astype(BF16).reshape(pieces, PIECE, D)
        u_ref[here, 48:64, :] = kv.astype(BF16).reshape(pieces, PIECE, D)
        u_ref[here, 0:16, :] = both[:, :D].astype(BF16).reshape(pieces, PIECE, D)
        if h == 0:
            cached.wait()
        copy = pltpu.make_async_copy(u_ref.at[here, 0:64, :], u_any.at[here, 0:64, :], out_sem.at[h])
        copy.start()
        sent.append(copy)
        steer_sum = nn(high, g) + nn(low, g)
        tile = jnp.where(rows == h, jnp.broadcast_to(steer_sum, (8, D)), tile)
        vector = jnp.where(rows[:heads] == h, steer, 0.0).astype(BF16)
        gate = gate + nt(vector, g)
    u_ref[:, 64:72, :] = jnp.broadcast_to(tile.astype(BF16)[None], (u_ref.shape[0], 8, D))
    copy = pltpu.make_async_copy(u_ref.at[:, 64:72, :], u_any.at[:, 64:72, :], out_sem.at[heads])
    copy.start()
    sent.append(copy)
    gate_ref[...] = jnp.sum(gate, axis=0, keepdims=True)
    for copy in sent:
        copy.wait()


def block_sums(queries, key_rows, value_rows, out_grad, cache_states, session_start, probe_gate, steer_vector):
    length, width = queries.shape
    heads = width // D
    total = heads * D // PIECE
    near = pltpu.VMEM((heads, length, D), BF16)
    hbm, vmem = whole(pltpu.HBM), whole(pltpu.VMEM)
    return pl.pallas_call(
        sums_kernel,
        in_specs=[hbm] * 8,
        out_specs=[hbm, vmem],
        out_shape=[
            jax.ShapeDtypeStruct((total, 72, D), BF16),
            jax.ShapeDtypeStruct((1, length), F32),
        ],
        scratch_shapes=[
            pltpu.SMEM(session_start.shape, jnp.int32),
            near,
            near,
            near,
            near,
            pltpu.VMEM((1, length), F32),
            pltpu.VMEM(steer_vector.shape, BF16),
            pltpu.VMEM((total, 72, D), BF16),
            pltpu.SemaphoreType.DMA((4, heads)),
            pltpu.SemaphoreType.DMA((4,)),
            pltpu.SemaphoreType.DMA((heads + 1,)),
        ],
        compiler_params=pltpu.CompilerParams(vmem_limit_bytes=VMEM_BYTES),
        cost_estimate=pl.CostEstimate(
            flops=8 * heads * length * D * D, bytes_accessed=8 * length * width, transcendentals=0
        ),
        name="block_sums",
    )(
        session_start,
        queries,
        key_rows,
        value_rows,
        out_grad,
        cache_states.reshape(total, PIECE, D),
        probe_gate.reshape(1, length),
        steer_vector,
    )


def scan_kernel(owner_any, v_any, w_any, steer_ref, owner_ref, v_ref, w_ref, in_sem, out_sem):
    blocks = v_ref.shape[0]
    fetched = [pltpu.make_async_copy(owner_any, owner_ref, in_sem.at[0])]
    for n, rows in enumerate((slice(16, 72), slice(0, 16))):
        fetched.append(pltpu.make_async_copy(v_any.at[:, rows, :], v_ref.at[:, rows, :], in_sem.at[n + 1]))
    for copy in fetched:
        copy.start()

    def begun_of(b):
        begun = v_ref[group_place(b, blocks), 16:32, :].astype(F32)
        return begun, begun < 0.5 * NONE

    state = jnp.zeros((PIECE, D), F32)
    steer = jnp.zeros((8, D), F32)
    for copy in fetched[:2]:
        copy.wait()
    for b in range(blocks):
        here = group_place(b, blocks)
        cached = v_ref[group_place(owner_ref[b], blocks), 32:48, :]
        w_ref[here, 0:16, :] = state.astype(BF16)
        w_ref[here, 16:32, :] = cached
        added = v_ref[here, 48:64, :].astype(F32)
        state = added + jnp.where(begun_of(b)[1], cached.astype(F32), state)
        steer = steer + v_ref[here, 64:72, :].astype(F32)
    first = pltpu.make_async_copy(w_ref.at[:, 0:32, :], w_any.at[:, 0:32, :], out_sem.at[0])
    first.start()
    for copy in fetched[2:]:
        copy.wait()
    state = jnp.zeros((PIECE, D), F32)
    for b in reversed(range(blocks)):
        here = group_place(b, blocks)
        begun, flag = begun_of(b)
        w_ref[here, 32:48, :] = state.astype(BF16)
        full = (begun + state) * (1.0 / D)
        slot = group_place(owner_ref[b], blocks)
        w_ref[slot, 48:64, :] = jnp.where(flag, full, 0.0).astype(BF16)
        state = v_ref[here, 0:16, :].astype(F32) + jnp.where(flag, 0.0, state)
    second = pltpu.make_async_copy(w_ref.at[:, 32:64, :], w_any.at[:, 32:64, :], out_sem.at[1])
    second.start()
    tokens = blocks * 1024
    steer_ref[...] = steer[0 : steer_ref.shape[0]] * (1.0 / math.sqrt(tokens))
    first.wait()
    second.wait()


def scan_blocks(owner, pieces, heads):
    blocks = pieces.shape[0]
    hbm, vmem = whole(pltpu.HBM), whole(pltpu.VMEM)
    return pl.pallas_call(
        scan_kernel,
        in_specs=[hbm, hbm],
        out_specs=[hbm, vmem],
        out_shape=[
            jax.ShapeDtypeStruct((blocks, 64, D), BF16),
            jax.ShapeDtypeStruct((heads, D), F32),
        ],
        scratch_shapes=[
            pltpu.SMEM(owner.shape, jnp.int32),
            pltpu.VMEM(pieces.shape, BF16),
            pltpu.VMEM((blocks, 64, D), BF16),
            pltpu.SemaphoreType.DMA((3,)),
            pltpu.SemaphoreType.DMA((2,)),
        ],
        compiler_params=pltpu.CompilerParams(vmem_limit_bytes=VMEM_BYTES),
        name="scan_blocks",
    )(owner, pieces)


def local_kernel(
    start_any, q_any, k_any, v_any, g_any, part_any,
    start_ref, q_ref, k_ref, v_ref, g_ref, sum_ref, part_ref, start_sem, in_sem, out_sem,
):
    heads, length, _ = q_ref.shape
    started = pltpu.make_async_copy(start_any, start_ref, start_sem)
    started.start()

    def fetches(h):
        pairs = ((g_any, g_ref), (v_any, v_ref), (k_any, k_ref), (q_any, q_ref))
        columns = pl.ds(pl.multiple_of(h * D, D), D)
        return [
            pltpu.make_async_copy(far.at[:, columns], near.at[h], in_sem.at[n, h])
            for n, (far, near) in enumerate(pairs)
        ]

    def result(h):
        return pltpu.make_async_copy(part_ref.at[:, h], part_any.at[:, h], out_sem.at[h])

    for h in range(AHEAD):
        for copy in fetches(h):
            copy.start()

    started.wait()
    start = start_ref[0]

    @pl.loop(0, heads)
    def _(h):
        for copy in fetches(h):
            copy.wait()

        @pl.when(h + AHEAD < heads)
        def _():
            for copy in fetches(h + AHEAD):
                copy.start()

        for i in range(length // STRIP):
            lo, hi = i * STRIP, (i + 1) * STRIP
            s = lo + lax.broadcasted_iota(jnp.int32, (STRIP, hi), 0)
            t = lax.broadcasted_iota(jnp.int32, (STRIP, hi), 1)
            keep = (t <= s) & (t >= jnp.where(s >= start, start, 0))
            g = g_ref[h, lo:hi, :]
            q = q_ref[h, lo:hi, :]
            y = jnp.where(keep, nt(g, v_ref[h, 0:hi, :]), 0.0).astype(BF16)
            part_ref[0, h, lo:hi, :] = nn(y, k_ref[h, 0:hi, :]).astype(BF16)
            x = jnp.where(keep, nt(q, k_ref[h, 0:hi, :]), 0.0).astype(BF16)
            dk = tn(y, q)
            dv = tn(x, g)
            sum_ref[0, lo:hi, :] = dk[lo:]
            sum_ref[1, lo:hi, :] = dv[lo:]
            if i > 0:
                sum_ref[0, 0:lo, :] += dk[:lo]
                sum_ref[1, 0:lo, :] += dv[:lo]
        part_ref[1, h] = sum_ref[0].astype(BF16)
        part_ref[2, h] = sum_ref[1].astype(BF16)
        result(h).start()

    for h in range(heads):
        result(h).wait()


def local_grads(session_start, queries, key_rows, value_rows, out_grad):
    length, width = queries.shape
    heads = width // D
    hbm = whole(pltpu.HBM)
    near = pltpu.VMEM((heads, length, D), BF16)
    return pl.pallas_call(
        local_kernel,
        in_specs=[hbm] * 5,
        out_specs=hbm,
        out_shape=jax.ShapeDtypeStruct((3, heads, length, D), BF16),
        scratch_shapes=[pltpu.SMEM(session_start.shape, jnp.int32)]
        + [near] * 4
        + [
            pltpu.VMEM((2, length, D), F32),
            pltpu.VMEM((3, heads, length, D), BF16),
            pltpu.SemaphoreType.DMA(()),
            pltpu.SemaphoreType.DMA((4, heads)),
            pltpu.SemaphoreType.DMA((heads,)),
        ],
        compiler_params=pltpu.CompilerParams(vmem_limit_bytes=VMEM_BYTES),
        cost_estimate=pl.CostEstimate(
            flops=16 * heads * length * length * D, bytes_accessed=20 * heads * length * D, transcendentals=0
        ),
        name="local_grads",
    )(session_start, queries, key_rows, value_rows, out_grad)


def state_kernel(
    start_any, k_ref, v_ref, g_ref, part_any, w_any,
    dq_any, dk_any, dv_any, dc_any,
    start_ref, part_ref, w_ref, out_ref, start_sem, in_sem, w_sem, c_sem, out_sem,
):
    _, heads, length, _ = part_ref.shape
    pieces = D // PIECE

    def fetch(h):
        return pltpu.make_async_copy(part_any.at[:, h], part_ref.at[:, h], in_sem.at[h])

    def states(h):
        here = slice(h * pieces, (h + 1) * pieces)
        return pltpu.make_async_copy(w_any.at[here], w_ref.at[here], w_sem.at[h])

    def cache(h):
        here = slice(h * pieces, (h + 1) * pieces)
        return pltpu.make_async_copy(w_ref.at[here, 48:64, :], dc_any.at[here], c_sem.at[h])

    started = pltpu.make_async_copy(start_any, start_ref, start_sem)
    started.start()
    for h in range(heads):
        states(h).start()
        fetch(h).start()
    copies = []
    started.wait()
    start = start_ref[0]
    before, after, final = row_masks(start, length)
    scale = 1.0 / D
    for h in range(heads):
        fetch(h).wait()
        states(h).wait()
        cache(h).start()
        copies.append(cache(h))
        columns = slice(h * D, (h + 1) * D)
        here = slice(h * pieces, (h + 1) * pieces)
        enter = w_ref[here, 0:16, :].reshape(D, D)
        cached = w_ref[here, 16:32, :].reshape(D, D)
        leave = w_ref[here, 32:48, :].reshape(D, D)
        g = g_ref[:, columns]
        inter = jnp.concatenate([g * before, g * after], axis=1)
        dq = part_ref[0, h].astype(F32) + nt(inter, jnp.concatenate([enter, cached], axis=1))
        out_ref[0, h] = (dq * scale).astype(BF16)
        dk = part_ref[1, h].astype(F32) + nt(v_ref[:, columns] * final, leave)
        out_ref[1, h] = (dk * scale).astype(BF16)
        dv = part_ref[2, h].astype(F32) + nn(k_ref[:, columns] * final, leave)
        out_ref[2, h] = (dv * scale).astype(BF16)
        for n, far in enumerate((dq_any, dk_any, dv_any)):
            copy = pltpu.make_async_copy(out_ref.at[n, h], far.at[:, columns], out_sem.at[n, h])
            copy.start()
            copies.append(copy)
    for copy in copies:
        copy.wait()


def state_grads(session_start, key_rows, value_rows, out_grad, parts, states):
    _, heads, length, _ = parts.shape
    total = heads * D // PIECE
    hbm, vmem = whole(pltpu.HBM), whole(pltpu.VMEM)
    near = pltpu.VMEM((3, heads, length, D), BF16)
    wide = jax.ShapeDtypeStruct((length, heads * D), BF16)
    *grads, grad_cache = pl.pallas_call(
        state_kernel,
        in_specs=[hbm, vmem, vmem, vmem, hbm, hbm],
        out_specs=[hbm] * 4,
        out_shape=[wide, wide, wide, jax.ShapeDtypeStruct((total, PIECE, D), BF16)],
        scratch_shapes=[
            pltpu.SMEM(session_start.shape, jnp.int32),
            near,
            pltpu.VMEM(states.shape, BF16),
            near,
            pltpu.SemaphoreType.DMA(()),
            pltpu.SemaphoreType.DMA((heads,)),
            pltpu.SemaphoreType.DMA((heads,)),
            pltpu.SemaphoreType.DMA((heads,)),
            pltpu.SemaphoreType.DMA((3, heads)),
        ],
        compiler_params=pltpu.CompilerParams(vmem_limit_bytes=STATE_BYTES),
        cost_estimate=pl.CostEstimate(
            flops=8 * heads * length * D * D, bytes_accessed=20 * heads * length * D, transcendentals=0
        ),
        name="state_grads",
    )(session_start, key_rows, value_rows, out_grad, parts, states)
    return *grads, grad_cache.reshape(1, heads, D, D)


def shards(
    queries,
    key_rows,
    value_rows,
    out_grad,
    cache_states,
    session_start,
    cache_owner,
    probe_gate,
    steer_vector,
):
    heads = steer_vector.shape[0]
    sent, gate = block_sums(
        queries, key_rows, value_rows, out_grad, cache_states, session_start, probe_gate, steer_vector
    )
    blocks = lax.axis_size("seq")
    group = [sorted(range(blocks), key=lambda b: group_place(b, blocks))]
    pieces = lax.all_to_all(sent, "seq", 0, 0, tiled=True, axis_index_groups=group)
    parts = local_grads(session_start, queries, key_rows, value_rows, out_grad)
    pieces, parts = lax.optimization_barrier((pieces, parts))
    scanned, grad_steer = scan_blocks(cache_owner, pieces, heads)
    states = lax.all_to_all(scanned, "seq", 0, 0, tiled=True, axis_index_groups=group)
    grad_queries, grad_keys, grad_values, grad_cache = state_grads(
        session_start, key_rows, value_rows, out_grad, parts, states
    )
    count = lax.axis_size("head")
    step = 1
    while step < count:
        gate = gate + lax.ppermute(gate, "head", [(i, i ^ step) for i in range(count)])
        step *= 2
    return (grad_queries, grad_keys, grad_values, grad_cache, grad_steer, gate.reshape(-1))


def solution(mesh):
    in_specs = (
        P("seq", "head"),
        P("seq", "head"),
        P("seq", "head"),
        P("seq", "head"),
        P("seq", "head", None, None),
        P("seq"),
        P(),
        P("seq"),
        P("head", None),
    )
    out_specs = (
        P("seq", "head"),
        P("seq", "head"),
        P("seq", "head"),
        P("seq", "head", None, None),
        P("head", None),
        P("seq"),
    )
    return jax.shard_map(shards, mesh=mesh, in_specs=in_specs, out_specs=out_specs, check_vma=False)
```
